32 devices in a mesh: dp: 4 (over y, x), space: 8 (over z, core).
Axes of the slice: x: 2, y: 2, z: 4, core: 2. Of those that a mesh axis runs over, the one named last changes fastest.
Arguments:
- signal: bfloat16 [4, 512, 64, 1280], P('dp', None, 'space'), may hold values from -6 to 6
- cotangent: bfloat16 [4, 512, 64, 1280], P('dp', None, 'space'), may hold values from -6 to 6
- spec_weight: bfloat16 [2, 20, 20, 73728], P(None, None, None, 'space'), may hold values from -1.25 to 1.25
- point_weight: bfloat16 [20, 20], replicated, may hold values from -1.25 to 1.25
- bias: bfloat16 [20], replicated, may hold values from -3 to 3
Outputs:
- grad_signal: bfloat16 [4, 512, 64, 1280], P('dp', None, 'space')
- spec_grad: float32 [2, 20, 20, 73728], P(None, None, None, ('space', 'dp'))
The draws below stay inside these ranges and needn't reach their ends.
All inputs are finite; a program needn't handle non-finite values.
Results may differ from the reference program's by a relative error of at most 0.024.
Values may be sent and summed in bfloat16 or wider, within the bound.
No kernel may reach another device: no remote copies, remote signals or barrier semaphores. Data moves between devices by JAX's collectives and lax.ppermute only.
A program may use at most 256 MiB of HBM per device.

```python
import math
import jax
import jax.numpy as jnp
from jax import lax

NX = 64
NY = 64
NZ = 32
NT = 16
C = 20
MX = 24
MY = 24
MZ = 16
MT = 8
SAMP_DEV = 1
SAMPLES = 4
MZT = 128
MODES = 73728
N_DP = 4


def levels(stream_key, extent, shards, least, largest):
    def one(dim, blocks):
        heights = jax.random.uniform(jax.random.fold_in(jax.random.fold_in(stream_key, 6), dim), (blocks,), jnp.float32, least / len(shards), largest / len(shards))
        return jnp.repeat(jnp.exp(heights), extent[dim] // blocks).reshape((-1,) + (1,) * (len(extent) - dim - 1))

    factor_of = one(*shards[0])
    for cut in shards[1:]:
        factor_of = factor_of * one(*cut)
    return factor_of


def bell_draw(stream_key, shape, spread, limit, shards=(), kind=jnp.bfloat16):
    array = jax.random.normal(stream_key, shape, jnp.float32) * spread
    if len(shards) > 0:
        array = levels(stream_key, shape, shards, -0.22, 0.18) * array
    return jnp.clip(array, min=-limit, max=limit).astype(kind)


def setup_inputs(seed: int = 0) -> dict:
    seeds = jax.random.split(jax.random.key(seed), 6)
    signal = bell_draw(seeds[0], (SAMPLES, NZ * NT, NX, C * NY), 1.0, 6.0, ((0, 4), (2, 8)))
    cotangent = bell_draw(seeds[1], (SAMPLES, NZ * NT, NX, C * NY), 1.0, 6.0, ((0, 4), (2, 8)))
    spec_weight = bell_draw(seeds[2], (2, C, C, MODES), C ** -0.5, 1.25, ((3, 8),))
    point_weight = bell_draw(seeds[3], (C, C), C ** -0.5, 1.25)
    bias = bell_draw(seeds[4], (C,), 0.5, 3.0)
    return {"signal": signal, "cotangent": cotangent, "spec_weight": spec_weight, "point_weight": point_weight, "bias": bias}


def retained(mode_count, length):
    positions = jnp.arange(mode_count, dtype=jnp.int32)
    return jnp.where(positions < mode_count // 2, positions, length - mode_count + positions)

def complex_table(mode_count, length):
    freqs = retained(mode_count, length)
    points = jnp.arange(length, dtype=jnp.int32)
    turns = freqs[:, None] * points[None, :] % length
    angles = turns.astype(jnp.float32) * (2.0 * math.pi / length)
    norm_scale = 1.0 / math.sqrt(length)
    cos_part = jnp.cos(angles) * norm_scale
    sin_part = jnp.sin(angles) * norm_scale
    upper_rows = jnp.stack([cos_part, sin_part], axis=1)
    lower_rows = jnp.stack([-sin_part, cos_part], axis=1)
    return jnp.stack([upper_rows, lower_rows], axis=0).astype(jnp.bfloat16)

def depth_tables():
    depth_freq = retained(MZ, NZ)
    time_freq = jnp.arange(MT, dtype=jnp.int32)
    depth_pos = jnp.arange(NZ, dtype=jnp.int32)
    time_pos = jnp.arange(NT, dtype=jnp.int32)
    depth_turns = depth_freq[:, None] * depth_pos[None, :] % NZ
    time_turns = time_freq[:, None] * time_pos[None, :] % NT
    turns = depth_turns[:, None, :, None] * NT + time_turns[None, :, None, :] * NZ
    angles = turns.astype(jnp.float32) * (2.0 * math.pi / (NZ * NT))
    norm_scale = 1.0 / math.sqrt(NZ * NT)
    forward = jnp.stack([jnp.cos(angles), -jnp.sin(angles)], axis=2) * norm_scale
    doubling = jnp.where(time_freq == 0, 1.0, 2.0).astype(jnp.float32)
    inverse = forward * doubling[None, :, None, None, None]
    return (forward.reshape(2 * MZT, NZ * NT).astype(jnp.bfloat16), inverse.reshape(2 * MZT, NZ * NT).astype(jnp.bfloat16))

def gelu_slope(pre_act):
    cumulative = 0.5 * (1.0 + lax.erf(pre_act * (1.0 / math.sqrt(2.0))))
    density = jnp.exp(-0.5 * pre_act * pre_act) * (1.0 / math.sqrt(2.0 * math.pi))
    return cumulative + pre_act * density

def fein(form, left, right):
    return jnp.einsum(form, left.astype(jnp.float32), right.astype(jnp.float32), precision=lax.Precision.HIGHEST)

def analyse(table_y, table_x, coeffs):
    values = coeffs.reshape(MZT, 2, NX, C, NY)
    after_y = fein('Pkpy,mpxcy->mPxck', table_y, values).astype(jnp.bfloat16)
    spectrum = fein('Pjpx,mpxck->Pcmjk', table_x, after_y).astype(jnp.bfloat16)
    return spectrum.reshape(2, C, MODES)

def synthesise(table_y, table_x, spectrum):
    unmerged = spectrum.reshape(2, C, MZT, MX, MY)
    after_x = fein('Pjpx,Pcmjk->mpxck', table_x, unmerged).astype(jnp.bfloat16)
    after_y = fein('Pkpy,mPxck->mpxcy', table_y, after_x).astype(jnp.bfloat16)
    return after_y.reshape(2 * MZT, NX * C * NY)

def reference(signal, cotangent, spec_weight, point_weight, bias):
    depth_table, depth_inverse = depth_tables()
    table_y = complex_table(MY, NY)
    table_x = complex_table(MX, NX)
    w_real = spec_weight[0]
    w_imag = spec_weight[1]

    def one_sample(inputs):
        sample_in, sample_cot = inputs
        coeffs = jnp.dot(depth_table, sample_in.reshape(NZ * NT, -1), preferred_element_type=jnp.float32).astype(jnp.bfloat16)
        u_hat = analyse(table_y, table_x, coeffs)
        v_real = fein('ik,iok->ok', u_hat[0], w_real) - fein('ik,iok->ok', u_hat[1], w_imag)
        v_imag = fein('ik,iok->ok', u_hat[1], w_real) + fein('ik,iok->ok', u_hat[0], w_imag)
        v_hat = jnp.stack([v_real, v_imag], axis=0).astype(jnp.bfloat16)
        synth = synthesise(table_y, table_x, v_hat)
        spectral = jnp.dot(depth_inverse.T, synth, preferred_element_type=jnp.float32).reshape(NZ * NT, NX, C, NY)
        unmerged = sample_in.reshape(NZ * NT, NX, C, NY)
        direct = fein('zxcy,co->zxoy', unmerged, point_weight)
        pre_act = spectral + direct + bias.astype(jnp.float32)[:, None]
        hidden = (sample_cot.reshape(NZ * NT, NX, C, NY).astype(jnp.float32) * gelu_slope(pre_act)).astype(jnp.bfloat16)
        e_coeffs = jnp.dot(depth_inverse, hidden.reshape(NZ * NT, -1), preferred_element_type=jnp.float32).astype(jnp.bfloat16)
        h_hat = analyse(table_y, table_x, e_coeffs)
        d_real = fein('ok,iok->ik', h_hat[0], w_real) + fein('ok,iok->ik', h_hat[1], w_imag)
        d_imag = fein('ok,iok->ik', h_hat[1], w_real) - fein('ok,iok->ik', h_hat[0], w_imag)
        d_hat = jnp.stack([d_real, d_imag], axis=0).astype(jnp.bfloat16)
        d_synth = synthesise(table_y, table_x, d_hat)
        returned = jnp.dot(depth_table.T, d_synth, preferred_element_type=jnp.float32).reshape(NZ * NT, NX, C, NY)
        grad = (returned + fein('zxoy,co->zxcy', hidden, point_weight)).astype(jnp.bfloat16)
        return (grad.reshape(NZ * NT, NX, C * NY), u_hat, h_hat)
    grads, u_hats, h_hats = lax.map(one_sample, (signal, cotangent))
    u_groups = u_hats.reshape(N_DP, SAMP_DEV, 2, C, MODES)
    h_groups = h_hats.reshape(N_DP, SAMP_DEV, 2, C, MODES)

    def group_term(summed, inputs):
        group_u, group_h = inputs
        real_part = fein('sik,sok->iok', group_u[:, 0], group_h[:, 0]) + fein('sik,sok->iok', group_u[:, 1], group_h[:, 1])
        imag_part = fein('sik,sok->iok', group_u[:, 0], group_h[:, 1]) - fein('sik,sok->iok', group_u[:, 1], group_h[:, 0])
        partial_value = jnp.stack([real_part, imag_part], axis=0)
        partial_value = lax.optimization_barrier(partial_value.astype(jnp.bfloat16)).astype(jnp.float32)
        return (summed + partial_value, None)
    start = jnp.zeros((2, C, C, MODES), jnp.float32)
    spec_grad, unused = lax.scan(group_term, start, (u_groups, h_groups))
    return (grads, spec_grad)
```

```python
import math

import jax
import jax.numpy as jnp
import ml_dtypes
import numpy as np
from jax import lax
from jax.sharding import PartitionSpec as P

NX = 64
NY = 64
NZ = 32
NT = 16
C = 20
MX = 24
MY = 24
MZ = 16
MT = 8
MZT = 128
BF = ml_dtypes.bfloat16


def retained(mode_count, length):
    positions = np.arange(mode_count)
    return np.where(positions < mode_count // 2, positions, length - mode_count + positions)


def complex_table(mode_count, length):
    freqs = retained(mode_count, length)
    turns = freqs[:, None] * np.arange(length)[None, :] % length
    angles = turns * (2.0 * math.pi / length)
    norm_scale = 1.0 / math.sqrt(length)
    cos_part = np.cos(angles) * norm_scale
    sin_part = np.sin(angles) * norm_scale
    upper_rows = np.stack([cos_part, sin_part], axis=1)
    lower_rows = np.stack([-sin_part, cos_part], axis=1)
    return np.stack([upper_rows, lower_rows], axis=0)


def depth_tables():
    depth_freq = retained(MZ, NZ)
    time_freq = np.arange(MT)
    depth_turns = depth_freq[:, None] * np.arange(NZ)[None, :] % NZ
    time_turns = time_freq[:, None] * np.arange(NT)[None, :] % NT
    turns = depth_turns[:, None, :, None] * NT + time_turns[None, :, None, :] * NZ
    angles = turns * (2.0 * math.pi / (NZ * NT))
    norm_scale = 1.0 / math.sqrt(NZ * NT)
    forward = np.stack([np.cos(angles), -np.sin(angles)], axis=2) * norm_scale
    doubling = np.where(time_freq == 0, 1.0, 2.0)
    inverse = forward * doubling[None, :, None, None, None]
    return forward.reshape(MZT, 2, NZ * NT).astype(BF), inverse.reshape(MZT, 2, NZ * NT).astype(BF)


def gelu_slope(pre_act):
    cumulative = 0.5 * (1.0 + lax.erf(pre_act * (1.0 / math.sqrt(2.0))))
    density = jnp.exp(-0.5 * pre_act * pre_act) * (1.0 / math.sqrt(2.0 * math.pi))
    return cumulative + pre_act * density


def block_table(table_y):
    blocks = np.einsum("cd,PjpY->pcYPdj", np.eye(C), table_y)
    return blocks.reshape(2, C * NY, 2 * C * MY).astype(BF)


def dot32(form, left, right):
    return jnp.einsum(form, left, right, preferred_element_type=jnp.float32)


def local(signal, cotangent, spec_weight, point_weight, bias):
    samples, depth_len, x_rows, merged = signal.shape
    depth_np, inverse_np = depth_tables()
    table_y = complex_table(MY, NY)
    table_x = jnp.asarray(complex_table(MX, NX).astype(BF))
    blocks = jnp.asarray(block_table(table_y))
    depth_table = jnp.asarray(depth_np)
    depth_inverse = jnp.asarray(inverse_np)
    point_block = (
        jnp.einsum("co,yz->cyoz", point_weight.astype(jnp.float32), jnp.eye(NY, dtype=jnp.float32))
        .reshape(C * NY, C * NY)
        .astype(jnp.bfloat16)
    )
    bias_row = jnp.repeat(bias.astype(jnp.float32), NY)
    w_real = spec_weight[0]
    w_imag = spec_weight[1]

    def analyse(table, grid_values):
        real = dot32("mz,szxr->smxr", table[:, 0], grid_values).astype(jnp.bfloat16)
        imag = dot32("mz,szxr->smxr", table[:, 1], grid_values).astype(jnp.bfloat16)
        both = dot32("smxr,rK->smxK", real, blocks[0]) + dot32("smxr,rK->smxK", imag, blocks[1])
        both = both.astype(jnp.bfloat16)
        moved = lax.all_to_all(both, "space", split_axis=1, concat_axis=2, tiled=True)
        halves = moved.reshape(samples, moved.shape[1], NX, 2, C * MY)
        total = dot32("Pipx,smxpr->sPmir", table_x, halves).astype(jnp.bfloat16)
        total = total.reshape(samples, 2, -1, MX, C, MY)
        return jnp.transpose(total, (0, 1, 4, 2, 3, 5)).reshape(samples, 2, C, -1)

    def synthesise(table, spectrum):
        unmerged = spectrum.reshape(samples, 2, C, -1, MX, MY)
        moved = jnp.transpose(unmerged, (0, 1, 3, 4, 2, 5)).reshape(samples, 2, -1, MX, C * MY)
        cells = dot32("Pipx,sPmir->smxpr", table_x, moved).astype(jnp.bfloat16)
        cells = cells.reshape(samples, cells.shape[1], NX, 2 * C * MY)
        back = lax.all_to_all(cells, "space", split_axis=2, concat_axis=1, tiled=True)
        real = dot32("smxK,rK->smxr", back, blocks[0]).astype(jnp.bfloat16)
        imag = dot32("smxK,rK->smxr", back, blocks[1]).astype(jnp.bfloat16)
        return dot32("mz,smxr->szxr", table[:, 0], real) + dot32("mz,smxr->szxr", table[:, 1], imag)

    direct = dot32("szxr,rR->szxR", signal, point_block)
    u_hat = analyse(depth_table, signal)
    v_real = dot32("sik,iok->sok", u_hat[:, 0], w_real) - dot32("sik,iok->sok", u_hat[:, 1], w_imag)
    v_imag = dot32("sik,iok->sok", u_hat[:, 1], w_real) + dot32("sik,iok->sok", u_hat[:, 0], w_imag)
    v_hat = jnp.stack([v_real, v_imag], axis=1).astype(jnp.bfloat16)
    pre_act = synthesise(depth_inverse, v_hat) + direct + bias_row
    hidden = (cotangent.astype(jnp.float32) * gelu_slope(pre_act)).astype(jnp.bfloat16)
    h_hat = analyse(depth_inverse, hidden)
    d_real = dot32("sok,iok->sik", h_hat[:, 0], w_real) + dot32("sok,iok->sik", h_hat[:, 1], w_imag)
    d_imag = dot32("sok,iok->sik", h_hat[:, 1], w_real) - dot32("sok,iok->sik", h_hat[:, 0], w_imag)
    d_hat = jnp.stack([d_real, d_imag], axis=1).astype(jnp.bfloat16)
    pointwise = dot32("szxR,rR->szxr", hidden, point_block)
    grad_signal = (synthesise(depth_table, d_hat) + pointwise).astype(jnp.bfloat16)
    u_all = lax.all_to_all(u_hat, "dp", split_axis=3, concat_axis=0, tiled=True)
    h_all = lax.all_to_all(h_hat, "dp", split_axis=3, concat_axis=0, tiled=True)
    u_all = u_all.astype(jnp.float32)
    h_all = h_all.astype(jnp.float32)

    def outer(left, right):
        return jnp.sum(left[:, :, None, :] * right[:, None, :, :], axis=0)

    grad_real = outer(u_all[:, 0], h_all[:, 0]) + outer(u_all[:, 1], h_all[:, 1])
    grad_imag = outer(u_all[:, 0], h_all[:, 1]) - outer(u_all[:, 1], h_all[:, 0])
    return (grad_signal, jnp.stack([grad_real, grad_imag], axis=0))


def solution(mesh):
    return jax.shard_map(
        local,
        mesh=mesh,
        in_specs=(
            P("dp", None, "space", None),
            P("dp", None, "space", None),
            P(None, None, None, "space"),
            P(),
            P(),
        ),
        out_specs=(P("dp", None, "space", None), P(None, None, None, ("space", "dp"))),
        check_vma=False,
    )
```

```python
import functools
import math

import jax
import jax.numpy as jnp
import ml_dtypes
import numpy as np
from jax import lax
from jax.experimental import pallas as pl
from jax.experimental.pallas import tpu as pltpu
from jax.sharding import PartitionSpec as P

NX = 64
NY = 64
NZ = 32
NT = 16
ZT = NZ * NT
C = 20
MX = 24
MY = 24
MZ = 16
MT = 8
MZT = 128
CY = C * NY
LANES = 512
KM = MX * MY
KB = 2 * KM
BF = ml_dtypes.bfloat16
BF16 = jnp.bfloat16
F32 = jnp.float32
VMEM_LIMIT = 56 * 1024 * 1024
PAIRS = ((0, 0), (0, 1), (1, 1), (1, 2), (2, 2), (2, 3), (3, 4))


def retained(mode_count, length):
    positions = np.arange(mode_count)
    return np.where(positions < mode_count // 2, positions, length - mode_count + positions)


def complex_table(mode_count, length):
    freqs = retained(mode_count, length)
    turns = freqs[:, None] * np.arange(length)[None, :] % length
    angles = turns * (2.0 * math.pi / length)
    norm_scale = 1.0 / math.sqrt(length)
    cos_part = np.cos(angles) * norm_scale
    sin_part = np.sin(angles) * norm_scale
    upper_rows = np.stack([cos_part, sin_part], axis=1)
    lower_rows = np.stack([-sin_part, cos_part], axis=1)
    return np.stack([upper_rows, lower_rows], axis=0)


def depth_tables():
    depth_freq = retained(MZ, NZ)
    time_freq = np.arange(MT)
    depth_turns = depth_freq[:, None] * np.arange(NZ)[None, :] % NZ
    time_turns = time_freq[:, None] * np.arange(NT)[None, :] % NT
    turns = depth_turns[:, None, :, None] * NT + time_turns[None, :, None, :] * NZ
    angles = turns * (2.0 * math.pi / ZT)
    norm_scale = 1.0 / math.sqrt(ZT)
    forward = np.stack([np.cos(angles), -np.sin(angles)], axis=2) * norm_scale
    doubling = np.where(time_freq == 0, 1.0, 2.0)
    inverse = forward * doubling[None, :, None, None, None]

    def square(table):
        real, imag = table.reshape(MZT, 2, ZT).transpose(1, 0, 2)
        return np.block([[real, -imag], [imag, real]]).astype(BF)

    return square(forward), square(inverse)


def y_tiles():
    table = complex_table(MY, NY)
    full = np.zeros((2, CY, LANES))
    for ch in range(C):
        full[:, ch * NY : (ch + 1) * NY, ch * MY : (ch + 1) * MY] = table[:, :, 0, :].transpose(0, 2, 1)
    tiles = []
    for tile, group in PAIRS:
        rows = full[:, 256 * group : 256 * group + 256, 128 * tile : 128 * tile + 128]
        tiles.append(np.concatenate([rows[0], rows[1]], axis=1))
    tiles = np.stack(tiles)
    return tiles.astype(BF), tiles.transpose(0, 2, 1).astype(BF)


def x_table(x_rows):
    table = complex_table(MX, NX)
    split = table.reshape(2, MX, 2, NX // x_rows, x_rows).transpose(3, 2, 4, 0, 1)
    out = np.zeros((NX // x_rows, 2, x_rows, 2, 4, 32))
    out[..., :MX] = split[:, :, :, :, None, :]
    return out.reshape(2 * NX, 256).astype(BF)


def lane_perms():
    perm = np.zeros((2, 768, 640))
    for i in range(MX):
        for j in range(MY):
            perm[:, 128 * (j // 4) + 32 * (j % 4) + i, i * MY + j] = 1.0
    perm[1] = np.roll(perm[1], 64, axis=1)
    return perm.astype(BF), perm.transpose(0, 2, 1).astype(BF)


def dot32(left, right):
    return jnp.dot(left, right, preferred_element_type=F32)


def forward_y(rows, yf_ref, y_scr):
    for tile in range(4):
        total = None
        for k, (pair_tile, group) in enumerate(PAIRS):
            if pair_tile == tile:
                part = dot32(rows[:, 256 * group : 256 * group + 256], yf_ref[k])
                total = part if total is None else total + part
        y_scr[2 * tile] = total[:, :128]
        y_scr[2 * tile + 1] = total[:, 128:]


def spread_x(y_scr, yt_scr, step, x_rows, depth_rows):
    start = pl.multiple_of(step * depth_rows, depth_rows)
    for x in range(x_rows):
        for tile in range(4):
            for part in range(2):
                piece = y_scr[2 * tile + part, pl.ds(x, depth_rows, stride=x_rows), :].astype(BF16)
                yt_scr[x, pl.ds(part * ZT + start, depth_rows), 128 * tile : 128 * tile + 128] = piece


def forward_depth(zf_ref, yt_scr, out_ref, x_rows):
    owners = out_ref.shape[0]
    modes_here = MZT // owners
    for x in range(x_rows):
        coeffs = dot32(zf_ref[...], yt_scr[x]).astype(BF16)
        for owner in range(owners):
            for part in range(2):
                row = part * MZT + owner * modes_here
                out_ref[owner, part, x] = coeffs[row : row + modes_here]


def inverse_depth(q_ref, zi_ref, z_scr, x_rows):
    owners = q_ref.shape[0]
    for x in range(x_rows):
        rows = jnp.concatenate([q_ref[owner, part, x] for part in range(2) for owner in range(owners)], axis=0)
        grid_rows = dot32(zi_ref[...], rows)
        for part in range(2):
            for tile in range(4):
                z_scr[2 * tile + part, pl.ds(x, ZT, stride=x_rows), :] = grid_rows[
                    part * ZT : (part + 1) * ZT, 128 * tile : 128 * tile + 128
                ]


def inverse_y(z_scr, yi_ref, start, count, group):
    total = None
    for k, (tile, pair_group) in enumerate(PAIRS):
        if pair_group == group:
            rows = jnp.concatenate([z_scr[2 * tile + p, pl.ds(start, count), :] for p in range(2)], axis=1)
            part = dot32(rows.astype(BF16), yi_ref[k])
            total = part if total is None else total + part
    return total


def gelu_slope(pre_act):
    size = jnp.abs(pre_act) * math.sqrt(0.5)
    gauss = jnp.exp(-(size * size))
    t = 1.0 / (1.0 + 0.3275911 * size)
    poly = t * (
        0.254829592 + t * (-0.284496736 + t * (1.421413741 + t * (-1.453152027 + t * 1.061405429)))
    )
    tail = 0.5 * poly * gauss
    cumulative = jnp.where(pre_act >= 0.0, 1.0 - tail, tail)
    return cumulative + pre_act * (gauss * (1.0 / math.sqrt(2.0 * math.pi)))


def analyse_kernel(s_ref, yf_ref, zf_ref, out_ref, y_scr, yt_scr, *, x_rows, depth_rows):
    step = pl.program_id(0)
    forward_y(s_ref[...], yf_ref, y_scr)
    spread_x(y_scr, yt_scr, step, x_rows, depth_rows)

    @pl.when(step == pl.num_programs(0) - 1)
    def _():
        forward_depth(zf_ref, yt_scr, out_ref, x_rows)


def middle_kernel(
    q_ref, d_ref, cot_ref, bias_ref, zi_ref, yi_ref, yf_ref, zf_ref, h_ref, out_ref,
    z_scr, pre_scr, y_scr, yt_scr, *, x_rows, depth_rows,
):
    step = pl.program_id(0)
    block = x_rows * depth_rows

    @pl.when(step == 0)
    def _():
        inverse_depth(q_ref, zi_ref, z_scr, x_rows)

    start = pl.multiple_of(step * block, block)
    for group in range(5):
        pre_scr[:, 256 * group : 256 * group + 256] = inverse_y(z_scr, yi_ref, start, block, group)

    def rows_body(index, carry):
        row = pl.multiple_of(index * 16, 16)
        for group in range(5):
            lanes = slice(256 * group, 256 * group + 256)
            pre_act = pre_scr[pl.ds(row, 16), lanes] + d_ref[pl.ds(row, 16), lanes].astype(F32) + bias_ref[:, lanes]
            hidden = cot_ref[pl.ds(row, 16), lanes].astype(F32) * gelu_slope(pre_act)
            h_ref[pl.ds(row, 16), lanes] = hidden.astype(BF16)
        return carry

    lax.fori_loop(0, block // 16, rows_body, 0)
    forward_y(h_ref[...], yf_ref, y_scr)
    spread_x(y_scr, yt_scr, step, x_rows, depth_rows)

    @pl.when(step == pl.num_programs(0) - 1)
    def _():
        forward_depth(zf_ref, yt_scr, out_ref, x_rows)


def final_kernel(q_ref, p_ref, zi_ref, yi_ref, out_ref, z_scr, *, x_rows, depth_rows):
    step = pl.program_id(0)
    block = x_rows * depth_rows

    @pl.when(step == 0)
    def _():
        inverse_depth(q_ref, zi_ref, z_scr, x_rows)

    start = pl.multiple_of(step * block, block)
    for group in range(5):
        lanes = slice(256 * group, 256 * group + 256)
        total = inverse_y(z_scr, yi_ref, start, block, group) + p_ref[:, lanes].astype(F32)
        out_ref[:, lanes] = total.astype(BF16)


def point_kernel(s_ref, b_ref, out_ref):
    out_ref[...] = dot32(s_ref[...], b_ref[...]).astype(BF16)


def mode_kernel(
    r_ref, w_ref, gx_ref, perm_ref, permt_ref, u_ref, q_ref,
    in_scr, out_scr, o_scr, ut_scr, u_scr, v_scr, vt_scr, *, backward,
):
    step = pl.program_id(0)
    owners, _, x_rows, modes_here, _ = r_ref.shape
    cells = 2 * NX
    slot = lax.broadcasted_iota(jnp.int32, (C, 128), 1) // 32

    @pl.when(step == 0)
    def _():
        o_scr[...] = jnp.zeros_like(o_scr)
        for owner in range(owners):
            rows = 2 * x_rows * modes_here
            values = r_ref[owner].reshape(rows, LANES).astype(F32)
            for tile in range(4):
                in_scr[tile, owner * rows : (owner + 1) * rows, :] = values[:, 128 * tile : 128 * tile + 128]

    for half in range(2):
        mode = 2 * step + half
        tiles = [in_scr[tile, pl.ds(mode, cells, stride=modes_here), :] for tile in range(4)]
        block = jnp.concatenate(tiles, axis=1).astype(BF16)
        cols = lax.dot_general(block, gx_ref[...], (((0,), (0,)), ((), ())), preferred_element_type=F32)
        for part in range(2):
            vt_scr[part] = cols[:, 128 * part : 128 * part + 128]
        for part in range(2):
            for a in range(6):
                piece = vt_scr[part, pl.ds(4 * a, C, stride=MY), :]
                for r in range(1, 4):
                    piece = jnp.where(slot == r, vt_scr[part, pl.ds(4 * a + r, C, stride=MY), :], piece)
                ut_scr[24 * part : 24 * part + C, 128 * a : 128 * a + 128] = piece
        moved = dot32(ut_scr[...].astype(BF16), perm_ref[half])
        for part in range(2):
            rows = moved[24 * part : 24 * part + C]
            if half == 0:
                u_scr[part, :C, :640] = rows
            else:
                u_scr[part, :C, 512:640] = u_scr[part, :C, 512:640] + rows[:, :128]
                u_scr[part, :C, 640:] = rows[:, 128:]
    for part in range(2):
        u_ref[part] = u_scr[part, :C, :].astype(BF16)

    for chunk in range(3):
        lanes = slice(384 * chunk, 384 * chunk + 384)
        if backward:
            real = u_scr[0, :C, lanes]
            imag = u_scr[1, :C, lanes]
            for ch in range(C):
                w_real = w_ref[0, ch, :, lanes].astype(F32)
                w_imag = w_ref[1, ch, :, lanes].astype(F32)
                v_scr[0, ch : ch + 1, lanes] = jnp.sum(w_real * real + w_imag * imag, axis=0, keepdims=True)
                v_scr[1, ch : ch + 1, lanes] = jnp.sum(w_real * imag - w_imag * real, axis=0, keepdims=True)
        else:
            real = jnp.zeros((C, 384), F32)
            imag = jnp.zeros((C, 384), F32)
            for ch in range(C):
                w_real = w_ref[0, ch, :, lanes].astype(F32)
                w_imag = w_ref[1, ch, :, lanes].astype(F32)
                u_real = u_scr[0, ch : ch + 1, lanes]
                u_imag = u_scr[1, ch : ch + 1, lanes]
                real = real + w_real * u_real - w_imag * u_imag
                imag = imag + w_real * u_imag + w_imag * u_real
            v_scr[0, :C, lanes] = real
            v_scr[1, :C, lanes] = imag

    for half in range(2):
        mode = 2 * step + half
        for part in range(2):
            rows = v_scr[part, :, 512 * half : 512 * half + 640].astype(BF16)
            moved = dot32(rows, permt_ref[half])
            for a in range(6):
                for r in range(4):
                    piece = jnp.where(slot == r, moved[:C, 128 * a : 128 * a + 128], 0.0)
                    o_scr[part, pl.ds(4 * a + r, C, stride=MY), :] = piece
        cols = jnp.concatenate([o_scr[0], o_scr[1]], axis=1).astype(BF16)
        back = lax.dot_general(gx_ref[...], cols, (((1,), (1,)), ((), ())), preferred_element_type=F32)
        for tile in range(4):
            out_scr[tile, pl.ds(mode, cells, stride=modes_here), :] = back[:, 128 * tile : 128 * tile + 128]

    @pl.when(step == pl.num_programs(0) - 1)
    def _():
        for owner in range(owners):
            rows = 2 * x_rows * modes_here
            for tile in range(4):
                values = out_scr[tile, owner * rows : (owner + 1) * rows, :].astype(BF16)
                q_ref[owner, :, :, :, 128 * tile : 128 * tile + 128] = values.reshape(2, x_rows, modes_here, 128)


def weight_kernel(u_ref, g_ref, out_ref):
    groups = u_ref.shape[0]
    width = u_ref.shape[3]
    lane_step = 384 if width % 384 == 0 else width
    for first in range(0, width, lane_step):
        lanes = slice(first, first + lane_step)
        real = jnp.zeros((C, lane_step), F32)
        imag = jnp.zeros((C, lane_step), F32)
        for group in range(groups):
            u_real = u_ref[group, 0, pl.ds(pl.program_id(0), 1), lanes]
            u_imag = u_ref[group, 1, pl.ds(pl.program_id(0), 1), lanes]
            g_real = g_ref[group, 0, :, lanes].astype(F32)
            g_imag = g_ref[group, 1, :, lanes].astype(F32)
            real = real + u_real * g_real + u_imag * g_imag
            imag = imag + u_real * g_imag - u_imag * g_real
        out_ref[0, 0, :, lanes] = real
        out_ref[1, 0, :, lanes] = imag


def whole(array):
    zeros = (0,) * len(array.shape)
    return pl.BlockSpec(array.shape, lambda i: zeros)


def params():
    return pltpu.CompilerParams(dimension_semantics=("arbitrary",), vmem_limit_bytes=VMEM_LIMIT)


def shape_of(shape, kind):
    return jax.ShapeDtypeStruct(shape, kind)


def local(signal, cotangent, spec_weight, point_weight, bias):
    samples, depth_len, x_rows, merged = signal.shape
    owners = NX // x_rows
    modes_here = MZT // owners
    modes = modes_here * KM
    dp_size = lax.axis_size("dp")
    share = modes // dp_size
    rows_all = ZT * x_rows
    depth_rows = 64
    block = depth_rows * x_rows
    steps = ZT // depth_rows

    forward_np, inverse_np = depth_tables()
    yf_np, yi_np = y_tiles()
    perm_np, permt_np = lane_perms()
    zf_fwd, zf_inv = jnp.asarray(forward_np), jnp.asarray(inverse_np)
    zi_fwd, zi_inv = jnp.asarray(forward_np.T.copy()), jnp.asarray(inverse_np.T.copy())
    yf, yi = jnp.asarray(yf_np), jnp.asarray(yi_np)
    perm, permt = jnp.asarray(perm_np), jnp.asarray(permt_np)
    gx = jnp.asarray(x_table(x_rows))
    spread = jnp.asarray((np.arange(CY)[:, None] // NY == np.arange(C)[None, :]).astype(BF))
    same_y = jnp.asarray(np.arange(NY)[:, None] == np.arange(NY)[None, :])

    sig = signal.reshape(rows_all, CY)
    cot = cotangent.reshape(rows_all, CY)
    payload = shape_of((owners, 2, x_rows, modes_here, LANES), BF16)
    row_spec = pl.BlockSpec((block, CY), lambda i: (i, 0))
    y_scr = pltpu.VMEM((8, block, 128), F32)
    yt_scr = pltpu.VMEM((x_rows, 2 * ZT, LANES), BF16)
    z_scr = pltpu.VMEM((8, rows_all, 128), F32)
    sizes = dict(x_rows=x_rows, depth_rows=depth_rows)

    def point_block(weights):
        wide = dot32(dot32(spread, weights).astype(BF16), spread.T)
        row_y = lax.broadcasted_iota(jnp.int32, (CY, CY), 0) % NY
        col_y = lax.broadcasted_iota(jnp.int32, (CY, CY), 1) % NY
        return jnp.where(row_y == col_y, wide, 0.0).astype(BF16)

    def point(values, weights):
        matrix = point_block(weights)
        return pl.pallas_call(
            point_kernel,
            grid=(steps,),
            in_specs=[row_spec, whole(matrix)],
            out_specs=row_spec,
            out_shape=shape_of((rows_all, CY), BF16),
            compiler_params=params(),
            name="point",
        )(values, matrix)

    def modes_call(received, backward):
        ints = modes_here // 2
        out_shape = (shape_of((2, C, modes), BF16), payload)
        return pl.pallas_call(
            functools.partial(mode_kernel, backward=backward),
            grid=(ints,),
            in_specs=[
                whole(received),
                pl.BlockSpec((2, C, C, KB), lambda i: (0, 0, 0, i)),
                whole(gx),
                whole(perm),
                whole(permt),
            ],
            out_specs=(pl.BlockSpec((2, C, KB), lambda i: (0, 0, i)), whole(payload)),
            out_shape=out_shape,
            scratch_shapes=[
                pltpu.VMEM((4, 2 * NX * modes_here, 128), F32),
                pltpu.VMEM((4, 2 * NX * modes_here, 128), F32),
                pltpu.VMEM((2, LANES, 128), F32),
                pltpu.VMEM((48, 768), F32),
                pltpu.VMEM((2, 24, KB), F32),
                pltpu.VMEM((2, 24, KB), F32),
                pltpu.VMEM((2, LANES, 128), F32),
            ],
            compiler_params=params(),
            name="modes",
        )(received, spec_weight, gx, perm, permt)

    def exchange(values):
        return lax.all_to_all(values, "space", split_axis=0, concat_axis=0, tiled=True)

    def to_owners(spectrum):
        cut = jnp.transpose(spectrum.reshape(2, C, dp_size, share), (2, 0, 1, 3))
        return lax.all_to_all(cut, "dp", split_axis=0, concat_axis=0, tiled=True)

    coeffs = pl.pallas_call(
        functools.partial(analyse_kernel, **sizes),
        grid=(steps,),
        in_specs=[row_spec, whole(yf), whole(zf_fwd)],
        out_specs=whole(payload),
        out_shape=payload,
        scratch_shapes=[y_scr, yt_scr],
        compiler_params=params(),
        name="analyse",
    )(sig, yf, zf_fwd)
    u_hat, v_cells = modes_call(exchange(coeffs), False)
    direct = point(sig, point_weight)
    bias_row = jnp.repeat(bias.astype(F32), NY).reshape(1, CY)
    v_here = exchange(v_cells)
    hidden, e_coeffs = pl.pallas_call(
        functools.partial(middle_kernel, **sizes),
        grid=(steps,),
        in_specs=[
            whole(payload), row_spec, row_spec, whole(bias_row), whole(zi_inv), whole(yi), whole(yf), whole(zf_inv),
        ],
        out_specs=(row_spec, whole(payload)),
        out_shape=(shape_of((rows_all, CY), BF16), payload),
        scratch_shapes=[z_scr, pltpu.VMEM((block, CY), F32), y_scr, yt_scr],
        compiler_params=params(),
        name="middle",
    )(v_here, direct, cot, bias_row, zi_inv, yi, yf, zf_inv)
    pointwise = point(hidden, point_weight.T)
    g_hat, d_cells = modes_call(exchange(e_coeffs), True)
    d_here = exchange(d_cells)
    grad_signal = pl.pallas_call(
        functools.partial(final_kernel, **sizes),
        grid=(steps,),
        in_specs=[whole(payload), row_spec, whole(zi_fwd), whole(yi)],
        out_specs=row_spec,
        out_shape=shape_of((rows_all, CY), BF16),
        scratch_shapes=[z_scr],
        compiler_params=params(),
        name="final",
    )(d_here, pointwise, zi_fwd, yi)
    u_all = to_owners(u_hat).astype(F32)
    g_all = to_owners(g_hat)
    spec_grad = pl.pallas_call(
        weight_kernel,
        grid=(C,),
        in_specs=[whole(u_all), whole(g_all)],
        out_specs=pl.BlockSpec((2, 1, C, share), lambda i: (0, i, 0, 0)),
        out_shape=shape_of((2, C, C, share), F32),
        compiler_params=params(),
        name="weight",
    )(u_all, g_all)
    return (grad_signal.reshape(signal.shape), spec_grad)


def solution(mesh):
    return jax.shard_map(
        local,
        mesh=mesh,
        in_specs=(
            P("dp", None, "space", None),
            P("dp", None, "space", None),
            P(None, None, None, "space"),
            P(),
            P(),
        ),
        out_specs=(P("dp", None, "space", None), P(None, None, None, ("space", "dp"))),
        check_vma=False,
    )
```

```python
import functools
import math

import jax
import jax.numpy as jnp
import ml_dtypes
import numpy as np
from jax import lax
from jax.experimental import pallas as pl
from jax.experimental.pallas import tpu as pltpu
from jax.sharding import PartitionSpec as P

NX = 64
NY = 64
NZ = 32
NT = 16
ZT = NZ * NT
C = 20
MX = 24
MY = 24
MZ = 16
MT = 8
MZT = 128
CY = C * NY
LANES = 512
KM = MX * MY
KB = 2 * KM
BF = ml_dtypes.bfloat16
BF16 = jnp.bfloat16
F32 = jnp.float32
VMEM_LIMIT = 56 * 1024 * 1024
PAIRS = ((0, 0), (0, 1), (1, 1), (1, 2), (2, 2), (2, 3), (3, 4))


def retained(mode_count, length):
    positions = np.arange(mode_count)
    return np.where(positions < mode_count // 2, positions, length - mode_count + positions)


def complex_table(mode_count, length):
    freqs = retained(mode_count, length)
    turns = freqs[:, None] * np.arange(length)[None, :] % length
    angles = turns * (2.0 * math.pi / length)
    norm_scale = 1.0 / math.sqrt(length)
    cos_part = np.cos(angles) * norm_scale
    sin_part = np.sin(angles) * norm_scale
    upper_rows = np.stack([cos_part, sin_part], axis=1)
    lower_rows = np.stack([-sin_part, cos_part], axis=1)
    return np.stack([upper_rows, lower_rows], axis=0)


def depth_tables():
    depth_freq = retained(MZ, NZ)
    time_freq = np.arange(MT)
    depth_turns = depth_freq[:, None] * np.arange(NZ)[None, :] % NZ
    time_turns = time_freq[:, None] * np.arange(NT)[None, :] % NT
    turns = depth_turns[:, None, :, None] * NT + time_turns[None, :, None, :] * NZ
    angles = turns * (2.0 * math.pi / ZT)
    norm_scale = 1.0 / math.sqrt(ZT)
    forward = np.stack([np.cos(angles), -np.sin(angles)], axis=2) * norm_scale
    doubling = np.where(time_freq == 0, 1.0, 2.0)
    inverse = forward * doubling[None, :, None, None, None]

    def square(table):
        real, imag = table.reshape(MZT, 2, ZT).transpose(1, 0, 2)
        return np.block([[real, -imag], [imag, real]]).astype(BF)

    return square(forward), square(inverse)


def y_tiles():
    table = complex_table(MY, NY)
    full = np.zeros((2, CY, LANES))
    for ch in range(C):
        full[:, ch * NY : (ch + 1) * NY, ch * MY : (ch + 1) * MY] = table[:, :, 0, :].transpose(0, 2, 1)
    tiles = []
    for tile, group in PAIRS:
        rows = full[:, 256 * group : 256 * group + 256, 128 * tile : 128 * tile + 128]
        tiles.append(np.concatenate([rows[0], rows[1]], axis=1))
    tiles = np.stack(tiles)
    return tiles.astype(BF), tiles.transpose(0, 2, 1).astype(BF)


def x_table(x_rows):
    table = complex_table(MX, NX)
    split = table.reshape(2, MX, 2, NX // x_rows, x_rows).transpose(3, 2, 4, 0, 1)
    out = np.zeros((NX // x_rows, 2, x_rows, 2, 4, 32))
    out[..., :MX] = split[:, :, :, :, None, :]
    return out.reshape(2 * NX, 256).astype(BF)


def lane_perms():
    perm = np.zeros((2, 768, 640))
    for i in range(MX):
        for j in range(MY):
            perm[:, 128 * (j // 4) + 32 * (j % 4) + i, i * MY + j] = 1.0
    perm[1] = np.roll(perm[1], 64, axis=1)
    return perm.astype(BF), perm.transpose(0, 2, 1).astype(BF)


def dot32(left, right):
    return jnp.dot(left, right, preferred_element_type=F32)


def forward_y(rows, yf_ref, y_scr):
    for tile in range(4):
        total = None
        for k, (pair_tile, group) in enumerate(PAIRS):
            if pair_tile == tile:
                part = dot32(rows[:, 256 * group : 256 * group + 256], yf_ref[k])
                total = part if total is None else total + part
        y_scr[2 * tile] = total[:, :128]
        y_scr[2 * tile + 1] = total[:, 128:]


def spread_x(y_scr, yt_scr, step, x_rows, depth_rows):
    start = pl.multiple_of(step * depth_rows, depth_rows)
    for x in range(x_rows):
        for tile in range(4):
            for part in range(2):
                piece = y_scr[2 * tile + part, pl.ds(x, depth_rows, stride=x_rows), :].astype(BF16)
                yt_scr[x, pl.ds(part * ZT + start, depth_rows), 128 * tile : 128 * tile + 128] = piece


def forward_depth(zf_ref, yt_scr, out_ref, x_rows):
    owners = out_ref.shape[0]
    modes_here = MZT // owners
    for x in range(x_rows):
        coeffs = dot32(zf_ref[...], yt_scr[x]).astype(BF16)
        for owner in range(owners):
            for part in range(2):
                row = part * MZT + owner * modes_here
                out_ref[owner, part, x] = coeffs[row : row + modes_here]


def inverse_depth(q_ref, zi_ref, z_scr, x_rows):
    owners = q_ref.shape[0]
    for x in range(x_rows):
        rows = jnp.concatenate([q_ref[owner, part, x] for part in range(2) for owner in range(owners)], axis=0)
        grid_rows = dot32(zi_ref[...], rows)
        for part in range(2):
            for tile in range(4):
                z_scr[2 * tile + part, pl.ds(x, ZT, stride=x_rows), :] = grid_rows[
                    part * ZT : (part + 1) * ZT, 128 * tile : 128 * tile + 128
                ]


def inverse_y(z_scr, yi_ref, start, count, group):
    total = None
    for k, (tile, pair_group) in enumerate(PAIRS):
        if pair_group == group:
            rows = jnp.concatenate([z_scr[2 * tile + p, pl.ds(start, count), :] for p in range(2)], axis=1)
            part = dot32(rows.astype(BF16), yi_ref[k])
            total = part if total is None else total + part
    return total


def gelu_slope(pre_act):
    cumulative = 0.5 * (1.0 + lax.erf(pre_act * math.sqrt(0.5)))
    density = jnp.exp(-0.5 * pre_act * pre_act) * (1.0 / math.sqrt(2.0 * math.pi))
    return cumulative + pre_act * density


def analyse_kernel(s_ref, yf_ref, zf_ref, out_ref, y_scr, yt_scr, *, x_rows, depth_rows):
    step = pl.program_id(0)
    forward_y(s_ref[...], yf_ref, y_scr)
    spread_x(y_scr, yt_scr, step, x_rows, depth_rows)

    @pl.when(step == pl.num_programs(0) - 1)
    def _():
        forward_depth(zf_ref, yt_scr, out_ref, x_rows)


def middle_kernel(
    q_ref, d_ref, cot_ref, bias_ref, zi_ref, yi_ref, yf_ref, zf_ref, h_ref, out_ref,
    z_scr, y_scr, yt_scr, *, x_rows, depth_rows,
):
    step = pl.program_id(0)
    block = x_rows * depth_rows

    @pl.when(step == 0)
    def _():
        inverse_depth(q_ref, zi_ref, z_scr, x_rows)

    start = pl.multiple_of(step * block, block)
    for group in range(5):
        lanes = slice(256 * group, 256 * group + 256)
        total = inverse_y(z_scr, yi_ref, start, block, group)
        for first in range(0, block, 64):
            rows = slice(first, first + 64)
            pre_act = total[rows] + d_ref[rows, lanes].astype(F32) + bias_ref[:, lanes]
            hidden = cot_ref[rows, lanes].astype(F32) * gelu_slope(pre_act)
            h_ref[rows, lanes] = hidden.astype(BF16)
    forward_y(h_ref[...], yf_ref, y_scr)
    spread_x(y_scr, yt_scr, step, x_rows, depth_rows)

    @pl.when(step == pl.num_programs(0) - 1)
    def _():
        forward_depth(zf_ref, yt_scr, out_ref, x_rows)


def final_kernel(q_ref, p_ref, zi_ref, yi_ref, out_ref, z_scr, *, x_rows, depth_rows):
    step = pl.program_id(0)
    block = x_rows * depth_rows

    @pl.when(step == 0)
    def _():
        inverse_depth(q_ref, zi_ref, z_scr, x_rows)

    start = pl.multiple_of(step * block, block)
    for group in range(5):
        lanes = slice(256 * group, 256 * group + 256)
        total = inverse_y(z_scr, yi_ref, start, block, group) + p_ref[:, lanes].astype(F32)
        out_ref[:, lanes] = total.astype(BF16)


def point_kernel(s_ref, b_ref, out_ref):
    out_ref[...] = dot32(s_ref[...], b_ref[...]).astype(BF16)


def mode_kernel(
    r_ref, w_ref, gx_ref, perm_ref, permt_ref, u_ref, q_ref,
    in_scr, out_scr, o_scr, ut_scr, u_scr, v_scr, *, backward,
):
    step = pl.program_id(0)
    pairs = pl.num_programs(0)
    owners, _, x_rows, modes_here, _ = r_ref.shape
    count = modes_here // 2
    cells = 2 * NX
    rows = 2 * x_rows * modes_here
    slot = lax.broadcasted_iota(jnp.int32, (C, 128), 1) // 32

    @pl.when(step == 0)
    def _():
        for owner in range(owners):
            values = r_ref[owner].reshape(rows, LANES).astype(F32)
            for tile in range(4):
                in_scr[tile, owner * rows : (owner + 1) * rows, :] = values[:, 128 * tile : 128 * tile + 128]
        for mode in range(modes_here):
            pair, half = mode // 2, mode % 2
            tiles = [in_scr[tile, pl.ds(mode, cells, stride=modes_here), :] for tile in range(4)]
            block = jnp.concatenate(tiles, axis=1).astype(BF16)
            cols = lax.dot_general(block, gx_ref[...], (((0,), (0,)), ((), ())), preferred_element_type=F32)
            for part in range(2):
                here = 2 * (mode % 2) + part
                o_scr[here] = cols[:, 128 * part : 128 * part + 128]
                for a in range(6):
                    piece = o_scr[here, pl.ds(4 * a, C, stride=MY), :]
                    for r in range(1, 4):
                        piece = jnp.where(slot == r, o_scr[here, pl.ds(4 * a + r, C, stride=MY), :], piece)
                    ut_scr[half, pair, part, :C, 128 * a : 128 * a + 128] = piece
        even = dot32(ut_scr[0].reshape(count * 48, 768).astype(BF16), perm_ref[0])
        odd = dot32(ut_scr[1].reshape(count * 48, 768).astype(BF16), perm_ref[1])
        even = even.reshape(count, 2, 24, 640)
        odd = odd.reshape(count, 2, 24, 640)
        u_scr[:, :, :, :512] = even[:, :, :, :512]
        u_scr[:, :, :, 512:640] = even[:, :, :, 512:] + odd[:, :, :, :128]
        u_scr[:, :, :, 640:] = odd[:, :, :, 128:]

    for part in range(2):
        u_ref[0, part] = u_scr[step, part, :C, :].astype(BF16)
    for chunk in range(3):
        lanes = slice(384 * chunk, 384 * chunk + 384)
        if backward:
            real = u_scr[step, 0, :C, lanes]
            imag = u_scr[step, 1, :C, lanes]
            for ch in range(C):
                w_real = w_ref[0, ch, :, lanes].astype(F32)
                w_imag = w_ref[1, ch, :, lanes].astype(F32)
                v_scr[step, 0, ch : ch + 1, lanes] = jnp.sum(w_real * real + w_imag * imag, axis=0, keepdims=True)
                v_scr[step, 1, ch : ch + 1, lanes] = jnp.sum(w_real * imag - w_imag * real, axis=0, keepdims=True)
        else:
            real = jnp.zeros((C, 384), F32)
            imag = jnp.zeros((C, 384), F32)
            for ch in range(C):
                w_real = w_ref[0, ch, :, lanes].astype(F32)
                w_imag = w_ref[1, ch, :, lanes].astype(F32)
                u_real = u_scr[step, 0, ch : ch + 1, lanes]
                u_imag = u_scr[step, 1, ch : ch + 1, lanes]
                real = real + w_real * u_real - w_imag * u_imag
                imag = imag + w_real * u_imag + w_imag * u_real
            v_scr[step, 0, :C, lanes] = real
            v_scr[step, 1, :C, lanes] = imag

    @pl.when(step == pairs - 1)
    def _():
        for half in range(2):
            values = v_scr[:, :, :, 512 * half : 512 * half + 640].reshape(count * 48, 640).astype(BF16)
            ut_scr[half] = dot32(values, permt_ref[half]).reshape(count, 2, 24, 768)
        o_scr[...] = jnp.zeros_like(o_scr)
        for mode in range(modes_here):
            pair, half = mode // 2, mode % 2
            for part in range(2):
                here = 2 * half + part
                for a in range(6):
                    values = ut_scr[half, pair, part, :C, 128 * a : 128 * a + 128]
                    for r in range(4):
                        o_scr[here, pl.ds(4 * a + r, C, stride=MY), :] = jnp.where(slot == r, values, 0.0)
            cols = jnp.concatenate([o_scr[2 * half], o_scr[2 * half + 1]], axis=1).astype(BF16)
            back = lax.dot_general(gx_ref[...], cols, (((1,), (1,)), ((), ())), preferred_element_type=F32)
            for tile in range(4):
                out_scr[tile, pl.ds(mode, cells, stride=modes_here), :] = back[:, 128 * tile : 128 * tile + 128]
        for owner in range(owners):
            for tile in range(4):
                values = out_scr[tile, owner * rows : (owner + 1) * rows, :].astype(BF16)
                q_ref[owner, :, :, :, 128 * tile : 128 * tile + 128] = values.reshape(2, x_rows, modes_here, 128)


def weight_kernel(*refs):
    out_ref = refs[-1]
    pieces = refs[:-1]
    width = out_ref.shape[3]
    lane_step = 384 if width % 384 == 0 else width
    row = pl.ds(pl.program_id(0), 1)
    for first in range(0, width, lane_step):
        lanes = slice(first, first + lane_step)
        real = jnp.zeros((C, lane_step), F32)
        imag = jnp.zeros((C, lane_step), F32)
        for u_ref, g_ref in zip(pieces[::2], pieces[1::2]):
            u_real = u_ref[0, row, lanes]
            u_imag = u_ref[1, row, lanes]
            g_real = g_ref[0, :, lanes].astype(F32)
            g_imag = g_ref[1, :, lanes].astype(F32)
            real = real + u_real * g_real + u_imag * g_imag
            imag = imag + u_real * g_imag - u_imag * g_real
        out_ref[0, 0, :, lanes] = real
        out_ref[1, 0, :, lanes] = imag


def cost(micros):
    return pl.CostEstimate(flops=int(micros * 1e9), transcendentals=0, bytes_accessed=int(micros * 3e6))


def whole(array):
    zeros = (0,) * len(array.shape)
    return pl.BlockSpec(array.shape, lambda i: zeros)


def params():
    return pltpu.CompilerParams(dimension_semantics=("arbitrary",), vmem_limit_bytes=VMEM_LIMIT)


def shape_of(shape, kind):
    return jax.ShapeDtypeStruct(shape, kind)


def local(signal, cotangent, spec_weight, point_weight, bias):
    samples, depth_len, x_rows, merged = signal.shape
    owners = NX // x_rows
    modes_here = MZT // owners
    modes = modes_here * KM
    dp_size = lax.axis_size("dp")
    share = modes // dp_size
    rows_all = ZT * x_rows
    depth_rows = 128
    block = depth_rows * x_rows
    steps = ZT // depth_rows

    forward_np, inverse_np = depth_tables()
    yf_np, yi_np = y_tiles()
    perm_np, permt_np = lane_perms()
    zf_fwd, zf_inv = jnp.asarray(forward_np), jnp.asarray(inverse_np)
    zi_fwd, zi_inv = jnp.asarray(forward_np.T.copy()), jnp.asarray(inverse_np.T.copy())
    yf, yi = jnp.asarray(yf_np), jnp.asarray(yi_np)
    perm, permt = jnp.asarray(perm_np), jnp.asarray(permt_np)
    gx = jnp.asarray(x_table(x_rows))
    spread = jnp.asarray((np.arange(CY)[:, None] // NY == np.arange(C)[None, :]).astype(BF))
    same_y = jnp.asarray(np.arange(NY)[:, None] == np.arange(NY)[None, :])

    sig = signal.reshape(rows_all, CY)
    cot = cotangent.reshape(rows_all, CY)
    payload = shape_of((owners, 2, x_rows, modes_here, LANES), BF16)
    row_spec = pl.BlockSpec((block, CY), lambda i: (i, 0))
    y_scr = pltpu.VMEM((8, block, 128), F32)
    yt_scr = pltpu.VMEM((x_rows, 2 * ZT, LANES), BF16)
    z_scr = pltpu.VMEM((8, rows_all, 128), F32)
    sizes = dict(x_rows=x_rows, depth_rows=depth_rows)

    def point_block(weights):
        wide = dot32(dot32(spread, weights).astype(BF16), spread.T)
        row_y = lax.broadcasted_iota(jnp.int32, (CY, CY), 0) % NY
        col_y = lax.broadcasted_iota(jnp.int32, (CY, CY), 1) % NY
        return jnp.where(row_y == col_y, wide, 0.0).astype(BF16)

    def point(values, weights):
        matrix = point_block(weights)
        return pl.pallas_call(
            point_kernel,
            grid=(steps,),
            in_specs=[row_spec, whole(matrix)],
            out_specs=row_spec,
            out_shape=shape_of((rows_all, CY), BF16),
            compiler_params=params(), cost_estimate=cost(18),
            name="point",
        )(values, matrix)

    aligned = share % KB == 0

    def modes_call(received, backward):
        pairs = modes_here // 2
        if aligned:
            per = share // KB
            u_shape = shape_of((dp_size, 2, C, share), BF16)
            u_spec = pl.BlockSpec((1, 2, C, KB), lambda i: (i // per, 0, 0, i % per))
        else:
            u_shape = shape_of((1, 2, C, modes), BF16)
            u_spec = pl.BlockSpec((1, 2, C, KB), lambda i: (0, 0, 0, i))
        return pl.pallas_call(
            functools.partial(mode_kernel, backward=backward),
            grid=(pairs,),
            in_specs=[
                whole(received),
                pl.BlockSpec((2, C, C, KB), lambda i: (0, 0, 0, i)),
                whole(gx),
                whole(perm),
                whole(permt),
            ],
            out_specs=(u_spec, whole(payload)),
            out_shape=(u_shape, payload),
            scratch_shapes=[
                pltpu.VMEM((4, 2 * NX * modes_here, 128), F32),
                pltpu.VMEM((4, 2 * NX * modes_here, 128), F32),
                pltpu.VMEM((4, LANES, 128), F32),
                pltpu.VMEM((2, pairs, 2, 24, 768), F32),
                pltpu.VMEM((pairs, 2, 24, KB), F32),
                pltpu.VMEM((pairs, 2, 24, KB), F32),
            ],
            compiler_params=params(), cost_estimate=cost(27),
            name="modes",
        )(received, spec_weight, gx, perm, permt)

    def exchange(values):
        return lax.all_to_all(values, "space", split_axis=0, concat_axis=0, tiled=True)

    me = lax.axis_index("dp")

    def to_owners(spectrum):
        if aligned:
            cut = spectrum
        else:
            cut = jnp.transpose(spectrum[0].reshape(2, C, dp_size, share), (2, 0, 1, 3))
        pieces = []
        for shift in range(dp_size):
            piece = lax.dynamic_index_in_dim(cut, (me + shift) % dp_size, 0, keepdims=False)
            if shift:
                piece = lax.ppermute(piece, "dp", [(i, (i + shift) % dp_size) for i in range(dp_size)])
            pieces.append(piece)
        return pieces

    coeffs = pl.pallas_call(
        functools.partial(analyse_kernel, **sizes),
        grid=(steps,),
        in_specs=[row_spec, whole(yf), whole(zf_fwd)],
        out_specs=whole(payload),
        out_shape=payload,
        scratch_shapes=[y_scr, yt_scr],
        compiler_params=params(), cost_estimate=cost(14),
        name="analyse",
    )(sig, yf, zf_fwd)
    direct = point(sig, point_weight)
    received, direct = lax.optimization_barrier((exchange(coeffs), direct))
    u_hat, v_cells = modes_call(received, False)
    bias_row = jnp.repeat(bias.astype(F32), NY).reshape(1, CY)
    u_pieces = [piece.astype(F32) for piece in to_owners(u_hat)]
    v_here, u_pieces = lax.optimization_barrier((exchange(v_cells), u_pieces))
    hidden, e_coeffs = pl.pallas_call(
        functools.partial(middle_kernel, **sizes),
        grid=(steps,),
        in_specs=[
            whole(payload), row_spec, row_spec, whole(bias_row), whole(zi_inv), whole(yi), whole(yf), whole(zf_inv),
        ],
        out_specs=(row_spec, whole(payload)),
        out_shape=(shape_of((rows_all, CY), BF16), payload),
        scratch_shapes=[z_scr, y_scr, yt_scr],
        compiler_params=params(), cost_estimate=cost(32),
        name="middle",
    )(v_here, direct, cot, bias_row, zi_inv, yi, yf, zf_inv)
    pointwise = point(hidden, point_weight.T)
    received, pointwise = lax.optimization_barrier((exchange(e_coeffs), pointwise))
    g_hat, d_cells = modes_call(received, True)
    d_here = exchange(d_cells)
    grad_signal = pl.pallas_call(
        functools.partial(final_kernel, **sizes),
        grid=(steps,),
        in_specs=[whole(payload), row_spec, whole(zi_fwd), whole(yi)],
        out_specs=row_spec,
        out_shape=shape_of((rows_all, CY), BF16),
        scratch_shapes=[z_scr],
        compiler_params=params(), cost_estimate=cost(16),
        name="final",
    )(d_here, pointwise, zi_fwd, yi)
    pieces = [piece for pair in zip(u_pieces, to_owners(g_hat)) for piece in pair]
    spec_grad = pl.pallas_call(
        weight_kernel,
        grid=(C,),
        in_specs=[whole(piece) for piece in pieces],
        out_specs=pl.BlockSpec((2, 1, C, share), lambda i: (0, i, 0, 0)),
        out_shape=shape_of((2, C, C, share), F32),
        compiler_params=params(), cost_estimate=cost(13),
        name="weight",
    )(*pieces)
    return (grad_signal.reshape(signal.shape), spec_grad)


def solution(mesh):
    return jax.shard_map(
        local,
        mesh=mesh,
        in_specs=(
            P("dp", None, "space", None),
            P("dp", None, "space", None),
            P(None, None, None, "space"),
            P(),
            P(),
        ),
        out_specs=(P("dp", None, "space", None), P(None, None, None, ("space", "dp"))),
        check_vma=False,
    )
```

```python
import functools
import math

import jax
import jax.numpy as jnp
import ml_dtypes
import numpy as np
from jax import lax
from jax.experimental import pallas as pl
from jax.experimental.pallas import tpu as pltpu
from jax.sharding import PartitionSpec as P

NX = 64
NY = 64
NZ = 32
NT = 16
ZT = NZ * NT
C = 20
MX = 24
MY = 24
MZ = 16
MT = 8
MZT = 128
CY = C * NY
LANES = 512
KM = MX * MY
KB = 2 * KM
BF = ml_dtypes.bfloat16
BF16 = jnp.bfloat16
F32 = jnp.float32
MIB = 1024 * 1024
PAIRS = ((0, 0), (0, 1), (1, 1), (1, 2), (2, 2), (2, 3), (3, 4))


def retained(mode_count, length):
    positions = np.arange(mode_count)
    return np.where(positions < mode_count // 2, positions, length - mode_count + positions)


def complex_table(mode_count, length):
    freqs = retained(mode_count, length)
    turns = freqs[:, None] * np.arange(length)[None, :] % length
    angles = turns * (2.0 * math.pi / length)
    norm_scale = 1.0 / math.sqrt(length)
    cos_part = np.cos(angles) * norm_scale
    sin_part = np.sin(angles) * norm_scale
    upper_rows = np.stack([cos_part, sin_part], axis=1)
    lower_rows = np.stack([-sin_part, cos_part], axis=1)
    return np.stack([upper_rows, lower_rows], axis=0)


def depth_tables():
    depth_freq = retained(MZ, NZ)
    time_freq = np.arange(MT)
    depth_turns = depth_freq[:, None] * np.arange(NZ)[None, :] % NZ
    time_turns = time_freq[:, None] * np.arange(NT)[None, :] % NT
    turns = depth_turns[:, None, :, None] * NT + time_turns[None, :, None, :] * NZ
    angles = turns * (2.0 * math.pi / ZT)
    norm_scale = 1.0 / math.sqrt(ZT)
    forward = np.stack([np.cos(angles), -np.sin(angles)], axis=2) * norm_scale
    doubling = np.where(time_freq == 0, 1.0, 2.0)
    inverse = forward * doubling[None, :, None, None, None]

    def square(table):
        real, imag = table.reshape(MZT, 2, ZT).transpose(1, 0, 2)
        return np.block([[real, -imag], [imag, real]]).astype(BF)

    return square(forward), square(inverse)


def y_tiles():
    table = complex_table(MY, NY)
    full = np.zeros((2, CY, LANES))
    for ch in range(C):
        full[:, ch * NY : (ch + 1) * NY, ch * MY : (ch + 1) * MY] = table[:, :, 0, :].transpose(0, 2, 1)
    tiles = []
    for tile, group in PAIRS:
        rows = full[:, 256 * group : 256 * group + 256, 128 * tile : 128 * tile + 128]
        tiles.append(np.concatenate([rows[0], rows[1]], axis=1))
    tiles = np.stack(tiles)
    return tiles.astype(BF), tiles.transpose(0, 2, 1).astype(BF)


def x_table(x_rows):
    table = complex_table(MX, NX)
    split = table.reshape(2, MX, 2, NX // x_rows, x_rows).transpose(3, 2, 4, 0, 1)
    out = np.zeros((NX // x_rows, 2, x_rows, 2, 2, 32))
    out[..., :MX] = split[:, :, :, :, None, :]
    return out.reshape(2 * NX, 128).astype(BF)


def lane_perms():
    perm = np.zeros((2, 768, 640))
    for i in range(MX):
        for j in range(MY):
            perm[:, 128 * (j // 4) + 32 * (j % 4) + i, i * MY + j] = 1.0
    perm[1] = np.roll(perm[1], 64, axis=1)
    return perm.astype(BF), perm.transpose(0, 2, 1).astype(BF)


def dot32(left, right):
    return jnp.dot(left, right, preferred_element_type=F32)


def forward_y(rows, yf_ref, y_scr):
    for tile in range(4):
        total = None
        for k, (pair_tile, group) in enumerate(PAIRS):
            if pair_tile == tile:
                part = dot32(rows[:, 256 * group : 256 * group + 256], yf_ref[k])
                total = part if total is None else total + part
        y_scr[2 * tile] = total[:, :128]
        y_scr[2 * tile + 1] = total[:, 128:]


def spread_x(y_scr, yt_scr, step, x_rows, depth_rows):
    start = pl.multiple_of(step * depth_rows, depth_rows)
    for x in range(x_rows):
        for tile in range(4):
            for part in range(2):
                piece = y_scr[2 * tile + part, pl.ds(x, depth_rows, stride=x_rows), :].astype(BF16)
                yt_scr[x, pl.ds(part * ZT + start, depth_rows), 128 * tile : 128 * tile + 128] = piece


def forward_depth(zf_ref, yt_scr, out_ref, x_rows):
    owners = out_ref.shape[0]
    modes_here = MZT // owners
    for x in range(x_rows):
        coeffs = dot32(zf_ref[...], yt_scr[x]).astype(BF16)
        for owner in range(owners):
            for part in range(2):
                row = part * MZT + owner * modes_here
                out_ref[owner, part, x] = coeffs[row : row + modes_here]


def inverse_depth(q_ref, zi_ref, z_scr, x_rows):
    owners = q_ref.shape[0]
    depth_rows = zi_ref.shape[1]
    table = jnp.concatenate([zi_ref[0], zi_ref[1]], axis=0)
    for x in range(x_rows):
        rows = jnp.concatenate([q_ref[owner, part, x] for part in range(2) for owner in range(owners)], axis=0)
        grid_rows = dot32(table, rows)
        for part in range(2):
            for tile in range(4):
                z_scr[2 * tile + part, pl.ds(x, depth_rows, stride=x_rows), :] = grid_rows[
                    part * depth_rows : (part + 1) * depth_rows, 128 * tile : 128 * tile + 128
                ]


def inverse_y(z_scr, yi_ref, group):
    total = None
    for k, (tile, pair_group) in enumerate(PAIRS):
        if pair_group == group:
            rows = jnp.concatenate([z_scr[2 * tile], z_scr[2 * tile + 1]], axis=1)
            part = dot32(rows.astype(BF16), yi_ref[k])
            total = part if total is None else total + part
    return total


def gelu_slope(pre_act):
    cumulative = 0.5 * (1.0 + lax.erf(pre_act * math.sqrt(0.5)))
    density = jnp.exp(-0.5 * pre_act * pre_act) * (1.0 / math.sqrt(2.0 * math.pi))
    return cumulative + pre_act * density


def analyse_kernel(s_ref, yf_ref, zf_ref, out_ref, y_scr, yt_scr, *, x_rows, depth_rows):
    step = pl.program_id(0)
    forward_y(s_ref[...], yf_ref, y_scr)
    spread_x(y_scr, yt_scr, step, x_rows, depth_rows)

    @pl.when(step == pl.num_programs(0) - 1)
    def _():
        forward_depth(zf_ref, yt_scr, out_ref, x_rows)


def middle_kernel(
    q_ref, d_ref, cot_ref, bias_ref, zi_ref, yi_ref, yf_ref, zf_ref, h_ref, out_ref,
    z_scr, y_scr, yt_scr, *, x_rows, depth_rows,
):
    step = pl.program_id(0)
    block = x_rows * depth_rows

    inverse_depth(q_ref, zi_ref, z_scr, x_rows)
    for group in range(5):
        lanes = slice(256 * group, 256 * group + 256)
        total = inverse_y(z_scr, yi_ref, group)
        for first in range(0, block, 64):
            rows = slice(first, first + 64)
            pre_act = total[rows] + d_ref[rows, lanes].astype(F32) + bias_ref[:, lanes]
            hidden = cot_ref[rows, lanes].astype(F32) * gelu_slope(pre_act)
            h_ref[rows, lanes] = hidden.astype(BF16)
    forward_y(h_ref[...], yf_ref, y_scr)
    spread_x(y_scr, yt_scr, step, x_rows, depth_rows)

    @pl.when(step == pl.num_programs(0) - 1)
    def _():
        forward_depth(zf_ref, yt_scr, out_ref, x_rows)


def final_kernel(q_ref, p_ref, zi_ref, yi_ref, out_ref, z_scr, *, x_rows):
    inverse_depth(q_ref, zi_ref, z_scr, x_rows)
    for group in range(5):
        lanes = slice(256 * group, 256 * group + 256)
        total = inverse_y(z_scr, yi_ref, group) + p_ref[:, lanes].astype(F32)
        out_ref[:, lanes] = total.astype(BF16)


def point_kernel(s_ref, b_ref, out_ref):
    out_ref[...] = dot32(s_ref[...], b_ref[...]).astype(BF16)


def mode_kernel(
    r_ref, w_ref, gx_ref, perm_ref, permt_ref, u_ref, q_ref,
    in_scr, out_scr, o_scr, ut_scr, u_scr, v_scr, *, backward,
):
    step = pl.program_id(0)
    pairs = pl.num_programs(0)
    owners, _, x_rows, modes_here, _ = r_ref.shape
    count = modes_here // 2
    cells = 2 * NX
    rows = 2 * x_rows * modes_here
    lane = lax.broadcasted_iota(jnp.int32, (C, 128), 1)
    odd_slot = lane // 32 % 2 == 1
    upper = lane >= 64

    @pl.when(step == 0)
    def _():
        for owner in range(owners):
            values = r_ref[owner].reshape(rows, LANES).astype(F32)
            for tile in range(4):
                in_scr[tile, owner * rows : (owner + 1) * rows, :] = values[:, 128 * tile : 128 * tile + 128]
        for mode in range(modes_here):
            pair, half = mode // 2, mode % 2
            tiles = [in_scr[tile, pl.ds(mode, cells, stride=modes_here), :] for tile in range(4)]
            block = jnp.concatenate(tiles, axis=1).astype(BF16)
            cols = lax.dot_general(block, gx_ref[...], (((0,), (0,)), ((), ())), preferred_element_type=F32)
            o_scr[half] = cols
            for a in range(6):
                pieces = [o_scr[half, pl.ds(4 * a + r, C, stride=MY), :] for r in range(4)]
                first = jnp.where(odd_slot, pieces[1], pieces[0])
                second = jnp.where(odd_slot, pieces[3], pieces[2])
                lanes = slice(128 * a, 128 * a + 128)
                ut_scr[half, pair, 0, :C, lanes] = jnp.where(upper, pltpu.roll(second, 64, 1), first)
                ut_scr[half, pair, 1, :C, lanes] = jnp.where(upper, second, pltpu.roll(first, 64, 1))
        even = dot32(ut_scr[0].reshape(count * 48, 768).astype(BF16), perm_ref[0])
        odd = dot32(ut_scr[1].reshape(count * 48, 768).astype(BF16), perm_ref[1])
        even = even.reshape(count, 2, 24, 640)
        odd = odd.reshape(count, 2, 24, 640)
        u_scr[:, :, :, :512] = even[:, :, :, :512]
        u_scr[:, :, :, 512:640] = even[:, :, :, 512:] + odd[:, :, :, :128]
        u_scr[:, :, :, 640:] = odd[:, :, :, 128:]

    for part in range(2):
        u_ref[0, part] = u_scr[step, part, :C, :].astype(BF16)
    for chunk in range(3):
        lanes = slice(384 * chunk, 384 * chunk + 384)
        if backward:
            real = u_scr[step, 0, :C, lanes]
            imag = u_scr[step, 1, :C, lanes]
            for ch in range(C):
                w_real = w_ref[0, ch, :, lanes].astype(F32)
                w_imag = w_ref[1, ch, :, lanes].astype(F32)
                v_scr[step, 0, ch : ch + 1, lanes] = jnp.sum(w_real * real + w_imag * imag, axis=0, keepdims=True)
                v_scr[step, 1, ch : ch + 1, lanes] = jnp.sum(w_real * imag - w_imag * real, axis=0, keepdims=True)
        else:
            real = jnp.zeros((C, 384), F32)
            imag = jnp.zeros((C, 384), F32)
            for ch in range(C):
                w_real = w_ref[0, ch, :, lanes].astype(F32)
                w_imag = w_ref[1, ch, :, lanes].astype(F32)
                u_real = u_scr[step, 0, ch : ch + 1, lanes]
                u_imag = u_scr[step, 1, ch : ch + 1, lanes]
                real = real + w_real * u_real - w_imag * u_imag
                imag = imag + w_real * u_imag + w_imag * u_real
            v_scr[step, 0, :C, lanes] = real
            v_scr[step, 1, :C, lanes] = imag

    @pl.when(step == pairs - 1)
    def _():
        for half in range(2):
            values = v_scr[:, :, :, 512 * half : 512 * half + 640].reshape(count * 48, 640).astype(BF16)
            ut_scr[half] = dot32(values, permt_ref[half]).reshape(count, 2, 24, 768)
        o_scr[...] = jnp.zeros_like(o_scr)
        for mode in range(modes_here):
            pair, half = mode // 2, mode % 2
            for a in range(6):
                lanes = slice(128 * a, 128 * a + 128)
                real = ut_scr[half, pair, 0, :C, lanes]
                imag = ut_scr[half, pair, 1, :C, lanes]
                first = jnp.where(upper, pltpu.roll(imag, 64, 1), real)
                second = jnp.where(upper, imag, pltpu.roll(real, 64, 1))
                for r, values in enumerate((first, first, second, second)):
                    kept = odd_slot if r % 2 else jnp.logical_not(odd_slot)
                    o_scr[half, pl.ds(4 * a + r, C, stride=MY), :] = jnp.where(kept, values, 0.0)
            back = lax.dot_general(
                gx_ref[...], o_scr[half].astype(BF16), (((1,), (1,)), ((), ())), preferred_element_type=F32
            )
            for tile in range(4):
                out_scr[tile, pl.ds(mode, cells, stride=modes_here), :] = back[:, 128 * tile : 128 * tile + 128]
        for owner in range(owners):
            for tile in range(4):
                values = out_scr[tile, owner * rows : (owner + 1) * rows, :].astype(BF16)
                q_ref[owner, :, :, :, 128 * tile : 128 * tile + 128] = values.reshape(2, x_rows, modes_here, 128)


def weight_kernel(*refs):
    out_ref = refs[-1]
    pieces = refs[:-1]
    width = out_ref.shape[3]
    lane_step = 384 if width % 384 == 0 else width
    row = pl.ds(pl.program_id(0), 1)
    for first in range(0, width, lane_step):
        lanes = slice(first, first + lane_step)
        real = jnp.zeros((C, lane_step), F32)
        imag = jnp.zeros((C, lane_step), F32)
        for u_ref, g_ref in zip(pieces[::2], pieces[1::2]):
            u_real = u_ref[0, row, lanes]
            u_imag = u_ref[1, row, lanes]
            g_real = g_ref[0, :, lanes].astype(F32)
            g_imag = g_ref[1, :, lanes].astype(F32)
            real = real + u_real * g_real + u_imag * g_imag
            imag = imag + u_real * g_imag - u_imag * g_real
        out_ref[0, 0, :, lanes] = real
        out_ref[1, 0, :, lanes] = imag


def cost(micros):
    return pl.CostEstimate(flops=int(micros * 1e9), transcendentals=0, bytes_accessed=int(micros * 3e6))


def whole(_):
    return pl.BlockSpec(memory_space=pltpu.VMEM)


def params(mebibytes=52):
    return pltpu.CompilerParams(dimension_semantics=("arbitrary",), vmem_limit_bytes=mebibytes * MIB)


def shape_of(shape, kind):
    return jax.ShapeDtypeStruct(shape, kind)


def local(signal, cotangent, spec_weight, point_weight, bias):
    samples, depth_len, x_rows, merged = signal.shape
    owners = NX // x_rows
    modes_here = MZT // owners
    modes = modes_here * KM
    dp_size = lax.axis_size("dp")
    share = modes // dp_size
    rows_all = ZT * x_rows
    depth_rows = 128
    block = depth_rows * x_rows
    steps = ZT // depth_rows

    forward_np, inverse_np = depth_tables()
    yf_np, yi_np = y_tiles()
    perm_np, permt_np = lane_perms()
    zf_fwd, zf_inv = jnp.asarray(forward_np), jnp.asarray(inverse_np)
    zi_fwd, zi_inv = jnp.asarray(forward_np.T.reshape(2, ZT, -1)), jnp.asarray(inverse_np.T.reshape(2, ZT, -1))
    yf, yi = jnp.asarray(yf_np), jnp.asarray(yi_np)
    perm, permt = jnp.asarray(perm_np), jnp.asarray(permt_np)
    gx = jnp.asarray(x_table(x_rows))
    spread = jnp.asarray((np.arange(CY)[:, None] // NY == np.arange(C)[None, :]).astype(BF))
    same_y = jnp.asarray(np.arange(NY)[:, None] == np.arange(NY)[None, :])

    sig = signal.reshape(rows_all, CY)
    cot = cotangent.reshape(rows_all, CY)
    payload = shape_of((owners, 2, x_rows, modes_here, LANES), BF16)
    payload_spec = pl.BlockSpec(payload.shape, lambda i: (0, 0, 0, 0, 0))
    zi_spec = pl.BlockSpec((2, depth_rows, 2 * MZT), lambda i: (0, i, 0))
    row_spec = pl.BlockSpec((block, CY), lambda i: (i, 0))
    y_scr = pltpu.VMEM((8, block, 128), F32)
    yt_scr = pltpu.VMEM((x_rows, 2 * ZT, LANES), BF16)
    z_scr = pltpu.VMEM((8, block, 128), F32)
    sizes = dict(x_rows=x_rows, depth_rows=depth_rows)

    def point_block(weights):
        wide = dot32(dot32(spread, weights).astype(BF16), spread.T)
        row_y = lax.broadcasted_iota(jnp.int32, (CY, CY), 0) % NY
        col_y = lax.broadcasted_iota(jnp.int32, (CY, CY), 1) % NY
        return jnp.where(row_y == col_y, wide, 0.0).astype(BF16)

    def point(values, weights):
        matrix = point_block(weights)
        return pl.pallas_call(
            point_kernel,
            grid=(steps,),
            in_specs=[row_spec, whole(matrix)],
            out_specs=row_spec,
            out_shape=shape_of((rows_all, CY), BF16),
            compiler_params=params(), cost_estimate=cost(18),
            name="point",
        )(values, matrix)

    aligned = share % KB == 0

    def modes_call(received, backward):
        pairs = modes_here // 2
        if aligned:
            per = share // KB
            u_shape = shape_of((dp_size, 2, C, share), BF16)
            u_spec = pl.BlockSpec((1, 2, C, KB), lambda i: (i // per, 0, 0, i % per))
        else:
            u_shape = shape_of((1, 2, C, modes), BF16)
            u_spec = pl.BlockSpec((1, 2, C, KB), lambda i: (0, 0, 0, i))
        return pl.pallas_call(
            functools.partial(mode_kernel, backward=backward),
            grid=(pairs,),
            in_specs=[
                whole(received),
                pl.BlockSpec((2, C, C, KB), lambda i: (0, 0, 0, i)),
                whole(gx),
                whole(perm),
                whole(permt),
            ],
            out_specs=(u_spec, payload_spec),
            out_shape=(u_shape, payload),
            scratch_shapes=[
                pltpu.VMEM((4, 2 * NX * modes_here, 128), F32),
                pltpu.VMEM((4, 2 * NX * modes_here, 128), F32),
                pltpu.VMEM((2, LANES, 128), F32),
                pltpu.VMEM((2, pairs, 2, 24, 768), F32),
                pltpu.VMEM((pairs, 2, 24, KB), F32),
                pltpu.VMEM((pairs, 2, 24, KB), F32),
            ],
            compiler_params=params(46), cost_estimate=cost(27),
            name="modes",
        )(received, spec_weight, gx, perm, permt)

    def exchange(values):
        return lax.all_to_all(values, "space", split_axis=0, concat_axis=0, tiled=True)

    me = lax.axis_index("dp")

    def to_owners(spectrum):
        if aligned:
            cut = spectrum
        else:
            cut = jnp.transpose(spectrum[0].reshape(2, C, dp_size, share), (2, 0, 1, 3))
        pieces = []
        for shift in range(dp_size):
            piece = lax.dynamic_index_in_dim(cut, (me + shift) % dp_size, 0, keepdims=False)
            if shift:
                piece = lax.ppermute(piece, "dp", [(i, (i + shift) % dp_size) for i in range(dp_size)])
            pieces.append(piece)
        return pieces

    coeffs = pl.pallas_call(
        functools.partial(analyse_kernel, **sizes),
        grid=(steps,),
        in_specs=[row_spec, whole(yf), whole(zf_fwd)],
        out_specs=payload_spec,
        out_shape=payload,
        scratch_shapes=[y_scr, yt_scr],
        compiler_params=params(), cost_estimate=cost(14),
        name="analyse",
    )(sig, yf, zf_fwd)
    direct = point(sig, point_weight)
    received, direct = lax.optimization_barrier((exchange(coeffs), direct))
    u_hat, v_cells = modes_call(received, False)
    bias_row = jnp.repeat(bias.astype(F32), NY).reshape(1, CY)
    u_pieces = [piece.astype(F32) for piece in to_owners(u_hat)]
    v_here, u_pieces = lax.optimization_barrier((exchange(v_cells), u_pieces))
    hidden, e_coeffs = pl.pallas_call(
        functools.partial(middle_kernel, **sizes),
        grid=(steps,),
        in_specs=[
            whole(payload), row_spec, row_spec, whole(bias_row), zi_spec, whole(yi), whole(yf), whole(zf_inv),
        ],
        out_specs=(row_spec, payload_spec),
        out_shape=(shape_of((rows_all, CY), BF16), payload),
        scratch_shapes=[z_scr, y_scr, yt_scr],
        compiler_params=params(), cost_estimate=cost(32),
        name="middle",
    )(v_here, direct, cot, bias_row, zi_inv, yi, yf, zf_inv)
    pointwise = point(hidden, point_weight.T)
    received, pointwise = lax.optimization_barrier((exchange(e_coeffs), pointwise))
    g_hat, d_cells = modes_call(received, True)
    d_here = exchange(d_cells)
    grad_signal = pl.pallas_call(
        functools.partial(final_kernel, x_rows=x_rows),
        grid=(steps,),
        in_specs=[whole(payload), row_spec, zi_spec, whole(yi)],
        out_specs=row_spec,
        out_shape=shape_of((rows_all, CY), BF16),
        scratch_shapes=[z_scr],
        compiler_params=params(), cost_estimate=cost(16),
        name="final",
    )(d_here, pointwise, zi_fwd, yi)
    pieces = [piece for pair in zip(u_pieces, to_owners(g_hat)) for piece in pair]
    spec_grad = pl.pallas_call(
        weight_kernel,
        grid=(C,),
        in_specs=[whole(piece) for piece in pieces],
        out_specs=pl.BlockSpec((2, 1, C, share), lambda i: (0, i, 0, 0)),
        out_shape=shape_of((2, C, C, share), F32),
        compiler_params=params(), cost_estimate=cost(13),
        name="weight",
    )(*pieces)
    return (grad_signal.reshape(signal.shape), spec_grad)


def solution(mesh):
    return jax.shard_map(
        local,
        mesh=mesh,
        in_specs=(
            P("dp", None, "space", None),
            P("dp", None, "space", None),
            P(None, None, None, "space"),
            P(),
            P(),
        ),
        out_specs=(P("dp", None, "space", None), P(None, None, None, ("space", "dp"))),
        check_vma=False,
    )
```

```python
import functools
import math

import jax
import jax.numpy as jnp
import ml_dtypes
import numpy as np
from jax import lax
from jax.experimental import pallas as pl
from jax.experimental.pallas import tpu as pltpu
from jax.sharding import PartitionSpec as P

NX = 64
NY = 64
NZ = 32
NT = 16
ZT = NZ * NT
C = 20
MX = 24
MY = 24
MZ = 16
MT = 8
MZT = 128
CY = C * NY
LANES = 512
CJ = C * MY
KM = MX * MY
KB = 2 * KM
BF = ml_dtypes.bfloat16
BF16 = jnp.bfloat16
F32 = jnp.float32
MIB = 1024 * 1024
PAIRS = ((0, 0), (0, 1), (1, 1), (1, 2), (2, 2), (2, 3), (3, 4))


def retained(mode_count, length):
    positions = np.arange(mode_count)
    return np.where(positions < mode_count // 2, positions, length - mode_count + positions)


def complex_table(mode_count, length):
    freqs = retained(mode_count, length)
    turns = freqs[:, None] * np.arange(length)[None, :] % length
    angles = turns * (2.0 * math.pi / length)
    norm_scale = 1.0 / math.sqrt(length)
    cos_part = np.cos(angles) * norm_scale
    sin_part = np.sin(angles) * norm_scale
    upper_rows = np.stack([cos_part, sin_part], axis=1)
    lower_rows = np.stack([-sin_part, cos_part], axis=1)
    return np.stack([upper_rows, lower_rows], axis=0)


def depth_tables():
    depth_freq = retained(MZ, NZ)
    time_freq = np.arange(MT)
    depth_turns = depth_freq[:, None] * np.arange(NZ)[None, :] % NZ
    time_turns = time_freq[:, None] * np.arange(NT)[None, :] % NT
    turns = depth_turns[:, None, :, None] * NT + time_turns[None, :, None, :] * NZ
    angles = turns * (2.0 * math.pi / ZT)
    norm_scale = 1.0 / math.sqrt(ZT)
    forward = np.stack([np.cos(angles), -np.sin(angles)], axis=2) * norm_scale
    doubling = np.where(time_freq == 0, 1.0, 2.0)
    inverse = forward * doubling[None, :, None, None, None]

    def square(table):
        real, imag = table.reshape(MZT, 2, ZT).transpose(1, 0, 2)
        return np.block([[real, -imag], [imag, real]]).astype(BF)

    return square(forward), square(inverse)


def y_tiles():
    table = complex_table(MY, NY)
    full = np.zeros((2, CY, LANES))
    for ch in range(C):
        full[:, ch * NY : (ch + 1) * NY, ch * MY : (ch + 1) * MY] = table[:, :, 0, :].transpose(0, 2, 1)
    tiles = []
    for tile, group in PAIRS:
        rows = full[:, 256 * group : 256 * group + 256, 128 * tile : 128 * tile + 128]
        tiles.append(np.concatenate([rows[0], rows[1]], axis=1))
    tiles = np.stack(tiles)
    return tiles.astype(BF), tiles.transpose(0, 2, 1).astype(BF)


def x_table(x_rows):
    table = complex_table(MX, NX)
    split = table.reshape(2, MX, 2, NX // x_rows, x_rows).transpose(3, 2, 4, 0, 1)
    out = np.zeros((NX // x_rows, 2, x_rows, 2, 2, 32))
    out[..., :MX] = split[:, :, :, :, None, :]
    return out.reshape(2 * NX, 128).astype(BF)


def lane_perms():
    perm = np.zeros((2, 768, 640))
    for i in range(MX):
        for j in range(MY):
            perm[:, 128 * (j // 4) + 32 * (j % 4) + i, i * MY + j] = 1.0
    perm[1] = np.roll(perm[1], 64, axis=1)
    return perm.astype(BF)


def dot32(left, right):
    return jnp.dot(left, right, preferred_element_type=F32)


def forward_y(rows, yf_ref, y_scr):
    for tile in range(4):
        total = None
        for k, (pair_tile, group) in enumerate(PAIRS):
            if pair_tile == tile:
                part = dot32(rows[:, 256 * group : 256 * group + 256], yf_ref[k])
                total = part if total is None else total + part
        y_scr[2 * tile] = total[:, :128]
        y_scr[2 * tile + 1] = total[:, 128:]


def spread_x(y_scr, yt_scr, step, x_rows, depth_rows):
    start = pl.multiple_of(step * depth_rows, depth_rows)
    for x in range(x_rows):
        for tile in range(4):
            for part in range(2):
                piece = y_scr[2 * tile + part, pl.ds(x, depth_rows, stride=x_rows), :].astype(BF16)
                yt_scr[x, pl.ds(part * ZT + start, depth_rows), 128 * tile : 128 * tile + 128] = piece


def forward_depth(zf_ref, yt_scr, out_ref, x_rows):
    owners, _, x_groups, modes_here, _ = out_ref.shape
    joined = x_rows // x_groups
    for x in range(x_rows):
        coeffs = dot32(zf_ref[...], yt_scr[x]).astype(BF16)
        lane = CJ * (x % joined)
        for owner in range(owners):
            for part in range(2):
                row = part * MZT + owner * modes_here
                out_ref[owner, part, x // joined, :, lane : lane + CJ] = coeffs[row : row + modes_here, :CJ]


def inverse_depth(q_ref, zi_ref, z_scr, x_rows):
    owners, _, x_groups, _, _ = q_ref.shape
    joined = x_rows // x_groups
    depth_rows = zi_ref.shape[1]
    margin = jnp.zeros((2 * MZT, LANES - CJ), BF16)
    table = jnp.concatenate([zi_ref[0], zi_ref[1]], axis=0)
    for x in range(x_rows):
        group, lanes = x // joined, slice(CJ * (x % joined), CJ * (x % joined) + CJ)
        rows = [q_ref[owner, part, group, :, lanes] for part in range(2) for owner in range(owners)]
        rows = jnp.concatenate([jnp.concatenate(rows, axis=0), margin], axis=1)
        grid_rows = dot32(table, rows)
        for part in range(2):
            for tile in range(4):
                z_scr[2 * tile + part, pl.ds(x, depth_rows, stride=x_rows), :] = grid_rows[
                    part * depth_rows : (part + 1) * depth_rows, 128 * tile : 128 * tile + 128
                ]


def inverse_y(z_scr, yi_ref, group):
    total = None
    for k, (tile, pair_group) in enumerate(PAIRS):
        if pair_group == group:
            rows = jnp.concatenate([z_scr[2 * tile], z_scr[2 * tile + 1]], axis=1)
            part = dot32(rows.astype(BF16), yi_ref[k])
            total = part if total is None else total + part
    return total


def twice_slope(pre_act):
    scaled = pre_act * math.sqrt(0.5)
    gauss = jnp.exp2(scaled * scaled * -math.log2(math.e))
    return (1.0 + lax.erf(scaled)) + (2.0 / math.sqrt(math.pi)) * scaled * gauss


def analyse_kernel(s_ref, yf_ref, zf_ref, out_ref, y_scr, yt_scr, *, x_rows, depth_rows):
    step = pl.program_id(0)
    forward_y(s_ref[...], yf_ref, y_scr)
    spread_x(y_scr, yt_scr, step, x_rows, depth_rows)

    @pl.when(step == pl.num_programs(0) - 1)
    def _():
        forward_depth(zf_ref, yt_scr, out_ref, x_rows)


def middle_kernel(
    q_ref, d_ref, cot_ref, bias_ref, zi_ref, yi_ref, yf_ref, zf_ref, h_ref, out_ref,
    z_scr, y_scr, yt_scr, *, x_rows, depth_rows,
):
    step = pl.program_id(0)
    block = x_rows * depth_rows

    inverse_depth(q_ref, zi_ref, z_scr, x_rows)
    for group in range(5):
        lanes = slice(256 * group, 256 * group + 256)
        total = inverse_y(z_scr, yi_ref, group)
        for first in range(0, block, 64):
            rows = slice(first, first + 64)
            pre_act = total[rows] + d_ref[rows, lanes].astype(F32) + bias_ref[:, lanes]
            hidden = (0.5 * cot_ref[rows, lanes].astype(F32)) * twice_slope(pre_act)
            h_ref[rows, lanes] = hidden.astype(BF16)
    forward_y(h_ref[...], yf_ref, y_scr)
    spread_x(y_scr, yt_scr, step, x_rows, depth_rows)

    @pl.when(step == pl.num_programs(0) - 1)
    def _():
        forward_depth(zf_ref, yt_scr, out_ref, x_rows)


def final_kernel(q_ref, p_ref, zi_ref, yi_ref, out_ref, z_scr, *, x_rows):
    inverse_depth(q_ref, zi_ref, z_scr, x_rows)
    for group in range(5):
        lanes = slice(256 * group, 256 * group + 256)
        total = inverse_y(z_scr, yi_ref, group) + p_ref[:, lanes].astype(F32)
        out_ref[:, lanes] = total.astype(BF16)


def point_kernel(s_ref, b_ref, out_ref):
    out_ref[...] = dot32(s_ref[...], b_ref[...]).astype(BF16)


def mode_kernel(
    r_ref, w_ref, gx_ref, perm_ref, u_ref, q_ref,
    in_scr, out_scr, o_scr, ut_scr, u_scr, v_scr, *, backward,
):
    step = pl.program_id(0)
    pairs = pl.num_programs(0)
    owners, _, x_groups, modes_here, width = r_ref.shape
    joined = width // CJ
    blocks = [(o, p, g, k) for o in range(owners) for p in range(2) for g in range(x_groups) for k in range(joined)]
    count = modes_here // 2
    cells = 2 * NX
    lane = lax.broadcasted_iota(jnp.int32, (C, 128), 1)
    odd_slot = lane // 32 % 2 == 1
    upper = lane >= 64

    @pl.when(step == 0)
    def _():
        for index, (owner, part, group, k) in enumerate(blocks):
            values = r_ref[owner, part, group, :, CJ * k : CJ * k + CJ].astype(F32)
            for tile in range(4):
                end = min(128 * tile + 128, CJ)
                in_scr[tile, index * modes_here : (index + 1) * modes_here, : end - 128 * tile] = values[
                    :, 128 * tile : end
                ]
        for mode in range(modes_here):
            pair, half = mode // 2, mode % 2
            tiles = [in_scr[tile, pl.ds(mode, cells, stride=modes_here), :] for tile in range(4)]
            block = jnp.concatenate(tiles, axis=1).astype(BF16)
            cols = lax.dot_general(block, gx_ref[...], (((0,), (0,)), ((), ())), preferred_element_type=F32)
            o_scr[half] = cols
            for a in range(6):
                pieces = [o_scr[half, pl.ds(4 * a + r, C, stride=MY), :] for r in range(4)]
                first = jnp.where(odd_slot, pieces[1], pieces[0])
                second = jnp.where(odd_slot, pieces[3], pieces[2])
                lanes = slice(128 * a, 128 * a + 128)
                ut_scr[half, pair, 0, :C, lanes] = jnp.where(upper, pltpu.roll(second, 64, 1), first)
                ut_scr[half, pair, 1, :C, lanes] = jnp.where(upper, second, pltpu.roll(first, 64, 1))
        even = dot32(ut_scr[0].reshape(count * 48, 768).astype(BF16), perm_ref[0])
        odd = dot32(ut_scr[1].reshape(count * 48, 768).astype(BF16), perm_ref[1])
        even = even.reshape(count, 2, 24, 640)
        odd = odd.reshape(count, 2, 24, 640)
        u_scr[:, :, :, :512] = even[:, :, :, :512]
        u_scr[:, :, :, 512:640] = even[:, :, :, 512:] + odd[:, :, :, :128]
        u_scr[:, :, :, 640:] = odd[:, :, :, 128:]

    for part in range(2):
        u_ref[0, part] = u_scr[step, part, :C, :].astype(BF16)
    for chunk in range(3):
        lanes = slice(384 * chunk, 384 * chunk + 384)
        if backward:
            real = u_scr[step, 0, :C, lanes]
            imag = u_scr[step, 1, :C, lanes]
            for ch in range(C):
                w_real = w_ref[0, ch, :, lanes].astype(F32)
                w_imag = w_ref[1, ch, :, lanes].astype(F32)
                v_scr[step, 0, ch : ch + 1, lanes] = jnp.sum(w_real * real + w_imag * imag, axis=0, keepdims=True)
                v_scr[step, 1, ch : ch + 1, lanes] = jnp.sum(w_real * imag - w_imag * real, axis=0, keepdims=True)
        else:
            real = jnp.zeros((C, 384), F32)
            imag = jnp.zeros((C, 384), F32)
            for ch in range(C):
                w_real = w_ref[0, ch, :, lanes].astype(F32)
                w_imag = w_ref[1, ch, :, lanes].astype(F32)
                u_real = u_scr[step, 0, ch : ch + 1, lanes]
                u_imag = u_scr[step, 1, ch : ch + 1, lanes]
                real = real + w_real * u_real - w_imag * u_imag
                imag = imag + w_real * u_imag + w_imag * u_real
            v_scr[step, 0, :C, lanes] = real
            v_scr[step, 1, :C, lanes] = imag

    @pl.when(step == pairs - 1)
    def _():
        for half in range(2):
            values = v_scr[:, :, :, 512 * half : 512 * half + 640].reshape(count * 48, 640).astype(BF16)
            moved = lax.dot_general(values, perm_ref[half], (((1,), (1,)), ((), ())), preferred_element_type=F32)
            ut_scr[half] = moved.reshape(count, 2, 24, 768)
        o_scr[...] = jnp.zeros_like(o_scr)
        for mode in range(modes_here):
            pair, half = mode // 2, mode % 2
            for a in range(6):
                lanes = slice(128 * a, 128 * a + 128)
                real = ut_scr[half, pair, 0, :C, lanes]
                imag = ut_scr[half, pair, 1, :C, lanes]
                first = jnp.where(upper, pltpu.roll(imag, 64, 1), real)
                second = jnp.where(upper, imag, pltpu.roll(real, 64, 1))
                for r, values in enumerate((first, first, second, second)):
                    kept = odd_slot if r % 2 else jnp.logical_not(odd_slot)
                    o_scr[half, pl.ds(4 * a + r, C, stride=MY), :] = jnp.where(kept, values, 0.0)
            back = lax.dot_general(
                gx_ref[...], o_scr[half].astype(BF16), (((1,), (1,)), ((), ())), preferred_element_type=F32
            )
            for tile in range(4):
                out_scr[tile, pl.ds(mode, cells, stride=modes_here), :] = back[:, 128 * tile : 128 * tile + 128]
        for index, (owner, part, group, k) in enumerate(blocks):
            rows = slice(index * modes_here, (index + 1) * modes_here)
            values = jnp.concatenate([out_scr[tile, rows, :] for tile in range(4)], axis=1)
            q_ref[owner, part, group, :, CJ * k : CJ * k + CJ] = values[:, :CJ].astype(BF16)


def weight_kernel(*refs):
    out_ref = refs[-1]
    pieces = refs[:-1]
    width = out_ref.shape[3]
    lane_step = 384 if width % 384 == 0 else width
    row = pl.ds(pl.program_id(0), 1)
    for first in range(0, width, lane_step):
        lanes = slice(first, first + lane_step)
        real = jnp.zeros((C, lane_step), F32)
        imag = jnp.zeros((C, lane_step), F32)
        for u_ref, g_ref in zip(pieces[::2], pieces[1::2]):
            u_real = u_ref[0, row, lanes]
            u_imag = u_ref[1, row, lanes]
            g_real = g_ref[0, :, lanes].astype(F32)
            g_imag = g_ref[1, :, lanes].astype(F32)
            real = real + u_real * g_real + u_imag * g_imag
            imag = imag + u_real * g_imag - u_imag * g_real
        out_ref[0, 0, :, lanes] = real
        out_ref[1, 0, :, lanes] = imag


def cost(micros):
    return pl.CostEstimate(flops=int(micros * 1e9), transcendentals=0, bytes_accessed=int(micros * 3e6))


def whole(_):
    return pl.BlockSpec(memory_space=pltpu.VMEM)


def fixed(array):
    zeros = (0,) * len(array.shape)
    return pl.BlockSpec(array.shape, lambda i: zeros)


def params(mebibytes=52):
    return pltpu.CompilerParams(dimension_semantics=("arbitrary",), vmem_limit_bytes=mebibytes * MIB)


def shape_of(shape, kind):
    return jax.ShapeDtypeStruct(shape, kind)


def local(signal, cotangent, spec_weight, point_weight, bias):
    samples, depth_len, x_rows, merged = signal.shape
    owners = NX // x_rows
    modes_here = MZT // owners
    modes = modes_here * KM
    dp_size = lax.axis_size("dp")
    share = modes // dp_size
    rows_all = ZT * x_rows
    depth_rows = 128
    block = depth_rows * x_rows
    steps = ZT // depth_rows

    forward_np, inverse_np = depth_tables()
    yf_np, yi_np = y_tiles()
    zf_fwd, zf_inv = jnp.asarray(forward_np), jnp.asarray(inverse_np)
    zi_fwd, zi_inv = jnp.asarray(forward_np.T.reshape(2, ZT, -1)), jnp.asarray(inverse_np.T.reshape(2, ZT, -1))
    yf, yi = jnp.asarray(yf_np), jnp.asarray(yi_np)
    perm = jnp.asarray(lane_perms())
    gx = jnp.asarray(x_table(x_rows))
    spread = jnp.asarray((np.arange(CY)[:, None] // NY == np.arange(C)[None, :]).astype(BF))
    same_y = jnp.asarray(np.arange(NY)[:, None] == np.arange(NY)[None, :])

    sig = signal.reshape(rows_all, CY)
    cot = cotangent.reshape(rows_all, CY)
    joined = math.gcd(x_rows, 4)
    payload = shape_of((owners, 2, x_rows // joined, modes_here, joined * CJ), BF16)
    payload_spec = pl.BlockSpec(payload.shape, lambda i: (0, 0, 0, 0, 0))
    zi_spec = pl.BlockSpec((2, depth_rows, 2 * MZT), lambda i: (0, i, 0))
    row_spec = pl.BlockSpec((block, CY), lambda i: (i, 0))
    y_scr = pltpu.VMEM((8, block, 128), F32)
    yt_scr = pltpu.VMEM((x_rows, 2 * ZT, LANES), BF16)
    z_scr = pltpu.VMEM((8, block, 128), F32)
    sizes = dict(x_rows=x_rows, depth_rows=depth_rows)

    def point_block(weights):
        wide = dot32(dot32(spread, weights).astype(BF16), spread.T)
        row_y = lax.broadcasted_iota(jnp.int32, (CY, CY), 0) % NY
        col_y = lax.broadcasted_iota(jnp.int32, (CY, CY), 1) % NY
        return jnp.where(row_y == col_y, wide, 0.0).astype(BF16)

    def point(values, weights):
        matrix = point_block(weights)
        return pl.pallas_call(
            point_kernel,
            grid=(steps,),
            in_specs=[row_spec, whole(matrix)],
            out_specs=row_spec,
            out_shape=shape_of((rows_all, CY), BF16),
            compiler_params=params(), cost_estimate=cost(18),
            name="point",
        )(values, matrix)

    aligned = share % KB == 0

    def modes_call(received, backward):
        pairs = modes_here // 2
        if aligned:
            per = share // KB
            u_shape = shape_of((dp_size, 2, C, share), BF16)
            u_spec = pl.BlockSpec((1, 2, C, KB), lambda i: (i // per, 0, 0, i % per))
        else:
            u_shape = shape_of((1, 2, C, modes), BF16)
            u_spec = pl.BlockSpec((1, 2, C, KB), lambda i: (0, 0, 0, i))
        return pl.pallas_call(
            functools.partial(mode_kernel, backward=backward),
            grid=(pairs,),
            in_specs=[
                whole(received),
                pl.BlockSpec((2, C, C, KB), lambda i: (0, 0, 0, i)),
                whole(gx),
                whole(perm),
            ],
            out_specs=(u_spec, payload_spec),
            out_shape=(u_shape, payload),
            scratch_shapes=[
                pltpu.VMEM((4, 2 * NX * modes_here, 128), F32),
                pltpu.VMEM((4, 2 * NX * modes_here, 128), F32),
                pltpu.VMEM((2, LANES, 128), F32),
                pltpu.VMEM((2, pairs, 2, 24, 768), F32),
                pltpu.VMEM((pairs, 2, 24, KB), F32),
                pltpu.VMEM((pairs, 2, 24, KB), F32),
            ],
            compiler_params=params(46), cost_estimate=cost(27),
            name="modes",
        )(received, spec_weight, gx, perm)

    def exchange(values):
        return lax.all_to_all(values, "space", split_axis=0, concat_axis=0, tiled=True)

    me = lax.axis_index("dp")

    def to_owners(spectrum):
        if aligned:
            cut = spectrum
        else:
            cut = jnp.transpose(spectrum[0].reshape(2, C, dp_size, share), (2, 0, 1, 3))
        pieces = []
        for shift in range(dp_size):
            piece = lax.dynamic_index_in_dim(cut, (me + shift) % dp_size, 0, keepdims=False)
            if shift:
                piece = lax.ppermute(piece, "dp", [(i, (i + shift) % dp_size) for i in range(dp_size)])
            pieces.append(piece)
        return pieces

    coeffs = pl.pallas_call(
        functools.partial(analyse_kernel, **sizes),
        grid=(steps,),
        in_specs=[row_spec, fixed(yf), fixed(zf_fwd)],
        out_specs=payload_spec,
        out_shape=payload,
        scratch_shapes=[y_scr, yt_scr],
        compiler_params=params(), cost_estimate=cost(14),
        name="analyse",
    )(sig, yf, zf_fwd)
    direct = point(sig, point_weight)
    received, direct = lax.optimization_barrier((exchange(coeffs), direct))
    u_hat, v_cells = modes_call(received, False)
    bias_row = jnp.repeat(bias.astype(F32), NY).reshape(1, CY)
    u_pieces = [piece.astype(F32) for piece in to_owners(u_hat)]
    v_here, u_pieces = lax.optimization_barrier((exchange(v_cells), u_pieces))
    hidden, e_coeffs = pl.pallas_call(
        functools.partial(middle_kernel, **sizes),
        grid=(steps,),
        in_specs=[
            whole(payload), row_spec, row_spec, whole(bias_row), zi_spec, whole(yi), whole(yf), fixed(zf_inv),
        ],
        out_specs=(row_spec, payload_spec),
        out_shape=(shape_of((rows_all, CY), BF16), payload),
        scratch_shapes=[z_scr, y_scr, yt_scr],
        compiler_params=params(), cost_estimate=cost(32),
        name="middle",
    )(v_here, direct, cot, bias_row, zi_inv, yi, yf, zf_inv)
    pointwise = point(hidden, point_weight.T)
    received, pointwise = lax.optimization_barrier((exchange(e_coeffs), pointwise))
    g_hat, d_cells = modes_call(received, True)
    d_here = exchange(d_cells)
    grad_signal = pl.pallas_call(
        functools.partial(final_kernel, x_rows=x_rows),
        grid=(steps,),
        in_specs=[whole(payload), row_spec, zi_spec, whole(yi)],
        out_specs=row_spec,
        out_shape=shape_of((rows_all, CY), BF16),
        scratch_shapes=[z_scr],
        compiler_params=params(), cost_estimate=cost(16),
        name="final",
    )(d_here, pointwise, zi_fwd, yi)
    pieces = [piece for pair in zip(u_pieces, to_owners(g_hat)) for piece in pair]
    spec_grad = pl.pallas_call(
        weight_kernel,
        grid=(C,),
        in_specs=[whole(piece) for piece in pieces],
        out_specs=pl.BlockSpec((2, 1, C, share), lambda i: (0, i, 0, 0)),
        out_shape=shape_of((2, C, C, share), F32),
        compiler_params=params(), cost_estimate=cost(13),
        name="weight",
    )(*pieces)
    return (grad_signal.reshape(signal.shape), spec_grad)


def solution(mesh):
    return jax.shard_map(
        local,
        mesh=mesh,
        in_specs=(
            P("dp", None, "space", None),
            P("dp", None, "space", None),
            P(None, None, None, "space"),
            P(),
            P(),
        ),
        out_specs=(P("dp", None, "space", None), P(None, None, None, ("space", "dp"))),
        check_vma=False,
    )
```

```python
import functools
import math

import jax
import jax.numpy as jnp
import ml_dtypes
import numpy as np
from jax import lax
from jax.experimental import pallas as pl
from jax.experimental.pallas import tpu as pltpu
from jax.sharding import PartitionSpec as P

NX = 64
NY = 64
NZ = 32
NT = 16
ZT = NZ * NT
C = 20
MX = 24
MY = 24
MZ = 16
MT = 8
MZT = 128
CY = C * NY
LANES = 512
CJ = C * MY
KM = MX * MY
KB = 2 * KM
PAIRS_STEP = 2
BF = ml_dtypes.bfloat16
BF16 = jnp.bfloat16
F32 = jnp.float32
MIB = 1024 * 1024
PAIRS = ((0, 0), (0, 1), (1, 1), (1, 2), (2, 2), (2, 3), (3, 4))


def retained(mode_count, length):
    positions = np.arange(mode_count)
    return np.where(positions < mode_count // 2, positions, length - mode_count + positions)


def complex_table(mode_count, length):
    freqs = retained(mode_count, length)
    turns = freqs[:, None] * np.arange(length)[None, :] % length
    angles = turns * (2.0 * math.pi / length)
    norm_scale = 1.0 / math.sqrt(length)
    cos_part = np.cos(angles) * norm_scale
    sin_part = np.sin(angles) * norm_scale
    upper_rows = np.stack([cos_part, sin_part], axis=1)
    lower_rows = np.stack([-sin_part, cos_part], axis=1)
    return np.stack([upper_rows, lower_rows], axis=0)


def depth_tables():
    depth_freq = retained(MZ, NZ)
    time_freq = np.arange(MT)
    depth_turns = depth_freq[:, None] * np.arange(NZ)[None, :] % NZ
    time_turns = time_freq[:, None] * np.arange(NT)[None, :] % NT
    turns = depth_turns[:, None, :, None] * NT + time_turns[None, :, None, :] * NZ
    angles = turns * (2.0 * math.pi / ZT)
    norm_scale = 1.0 / math.sqrt(ZT)
    forward = np.stack([np.cos(angles), -np.sin(angles)], axis=2) * norm_scale
    doubling = np.where(time_freq == 0, 1.0, 2.0)
    inverse = forward * doubling[None, :, None, None, None]

    def square(table):
        real, imag = table.reshape(MZT, 2, ZT).transpose(1, 0, 2)
        return np.block([[real, -imag], [imag, real]]).astype(BF)

    return square(forward), square(inverse)


def y_tiles():
    table = complex_table(MY, NY)
    full = np.zeros((2, CY, LANES))
    for ch in range(C):
        full[:, ch * NY : (ch + 1) * NY, ch * MY : (ch + 1) * MY] = table[:, :, 0, :].transpose(0, 2, 1)
    tiles = []
    for tile, group in PAIRS:
        rows = full[:, 256 * group : 256 * group + 256, 128 * tile : 128 * tile + 128]
        tiles.append(np.concatenate([rows[0], rows[1]], axis=1))
    tiles = np.stack(tiles)
    back = tiles.transpose(0, 2, 1)
    return tiles.astype(BF), back.astype(BF), (back * math.sqrt(0.5)).astype(BF)


def x_table(x_rows):
    table = complex_table(MX, NX)
    split = table.reshape(2, MX, 2, NX // x_rows, x_rows).transpose(3, 2, 4, 0, 1)
    out = np.zeros((NX // x_rows, 2, x_rows, 2, 2, 32))
    out[..., :MX] = split[:, :, :, :, None, :]
    return out.reshape(2 * NX, 128).astype(BF)


def lane_perms():
    perm = np.zeros((2, 768, 640))
    for i in range(MX):
        for j in range(MY):
            perm[:, 128 * (j // 4) + 32 * (j % 4) + i, i * MY + j] = 1.0
    perm[1] = np.roll(perm[1], 64, axis=1)
    return perm.astype(BF)


def dot32(left, right):
    return jnp.dot(left, right, preferred_element_type=F32)


def forward_y(rows, yf_ref, y_scr):
    for tile in range(4):
        total = None
        for k, (pair_tile, group) in enumerate(PAIRS):
            if pair_tile == tile:
                part = dot32(rows[:, 256 * group : 256 * group + 256], yf_ref[k])
                total = part if total is None else total + part
        y_scr[2 * tile] = total[:, :128]
        y_scr[2 * tile + 1] = total[:, 128:]


def spread_x(y_scr, yt_scr, step, x_rows, depth_rows):
    start = pl.multiple_of(step * depth_rows, depth_rows)
    for x in range(x_rows):
        for tile in range(4):
            for part in range(2):
                piece = y_scr[2 * tile + part, pl.ds(x, depth_rows, stride=x_rows), :].astype(BF16)
                yt_scr[x, pl.ds(part * ZT + start, depth_rows), 128 * tile : 128 * tile + 128] = piece


def forward_depth(zf_ref, yt_scr, out_ref, x_rows):
    owners, _, x_groups, modes_here, _ = out_ref.shape
    joined = x_rows // x_groups
    for x in range(x_rows):
        coeffs = dot32(zf_ref[...], yt_scr[x]).astype(BF16)
        lane = CJ * (x % joined)
        for owner in range(owners):
            for part in range(2):
                row = part * MZT + owner * modes_here
                out_ref[owner, part, x // joined, :, lane : lane + CJ] = coeffs[row : row + modes_here, :CJ]


def inverse_depth(q_ref, zi_ref, z_scr, x_rows):
    owners, _, x_groups, _, _ = q_ref.shape
    joined = x_rows // x_groups
    depth_rows = zi_ref.shape[1]
    margin = jnp.zeros((2 * MZT, LANES - CJ), BF16)
    table = jnp.concatenate([zi_ref[0], zi_ref[1]], axis=0)
    for x in range(x_rows):
        group, lanes = x // joined, slice(CJ * (x % joined), CJ * (x % joined) + CJ)
        rows = [q_ref[owner, part, group, :, lanes] for part in range(2) for owner in range(owners)]
        rows = jnp.concatenate([jnp.concatenate(rows, axis=0), margin], axis=1)
        grid_rows = dot32(table, rows)
        for part in range(2):
            for tile in range(4):
                z_scr[2 * tile + part, pl.ds(x, depth_rows, stride=x_rows), :] = grid_rows[
                    part * depth_rows : (part + 1) * depth_rows, 128 * tile : 128 * tile + 128
                ]


def inverse_y(z_scr, yi_ref, group):
    total = None
    for k, (tile, pair_group) in enumerate(PAIRS):
        if pair_group == group:
            rows = jnp.concatenate([z_scr[2 * tile], z_scr[2 * tile + 1]], axis=1)
            part = dot32(rows.astype(BF16), yi_ref[k])
            total = part if total is None else total + part
    return total


def twice_slope(scaled):
    gauss = jnp.exp2(scaled * scaled * -math.log2(math.e))
    return (1.0 + lax.erf(scaled)) + (2.0 / math.sqrt(math.pi)) * scaled * gauss


def analyse_kernel(s_ref, yf_ref, zf_ref, out_ref, y_scr, yt_scr, *, x_rows, depth_rows):
    step = pl.program_id(0)
    forward_y(s_ref[...], yf_ref, y_scr)
    spread_x(y_scr, yt_scr, step, x_rows, depth_rows)

    @pl.when(step == pl.num_programs(0) - 1)
    def _():
        forward_depth(zf_ref, yt_scr, out_ref, x_rows)


def middle_kernel(
    q_ref, d_ref, cot_ref, zi_ref, yi_ref, yf_ref, zf_ref, h_ref, out_ref,
    z_scr, y_scr, yt_scr, *, x_rows, depth_rows,
):
    step = pl.program_id(0)
    block = x_rows * depth_rows

    inverse_depth(q_ref, zi_ref, z_scr, x_rows)
    for group in range(5):
        lanes = slice(256 * group, 256 * group + 256)
        total = inverse_y(z_scr, yi_ref, group)
        for first in range(0, block, 64):
            rows = slice(first, first + 64)
            scaled = total[rows] + d_ref[rows, lanes].astype(F32)
            hidden = (0.5 * cot_ref[rows, lanes].astype(F32)) * twice_slope(scaled)
            h_ref[rows, lanes] = hidden.astype(BF16)
    forward_y(h_ref[...], yf_ref, y_scr)
    spread_x(y_scr, yt_scr, step, x_rows, depth_rows)

    @pl.when(step == pl.num_programs(0) - 1)
    def _():
        forward_depth(zf_ref, yt_scr, out_ref, x_rows)


def final_kernel(q_ref, p_ref, zi_ref, yi_ref, out_ref, z_scr, *, x_rows):
    inverse_depth(q_ref, zi_ref, z_scr, x_rows)
    for group in range(5):
        lanes = slice(256 * group, 256 * group + 256)
        total = inverse_y(z_scr, yi_ref, group) + p_ref[:, lanes].astype(F32)
        out_ref[:, lanes] = total.astype(BF16)


def point_kernel(s_ref, b_ref, out_ref):
    out_ref[...] = dot32(s_ref[...], b_ref[...]).astype(BF16)


def direct_kernel(s_ref, b_ref, bias_ref, out_ref):
    out_ref[...] = ((dot32(s_ref[...], b_ref[...]) + bias_ref[...]) * math.sqrt(0.5)).astype(BF16)


def mode_kernel(
    r_ref, w_ref, gx_ref, perm_ref, u_ref, q_ref,
    in_scr, out_scr, o_scr, ut_scr, u_scr, v_scr, *, backward,
):
    step = pl.program_id(0)
    steps = pl.num_programs(0)
    owners, _, x_groups, modes_here, width = r_ref.shape
    joined = width // CJ
    blocks = [(o, p, g, k) for o in range(owners) for p in range(2) for g in range(x_groups) for k in range(joined)]
    count = modes_here // 2
    cells = 2 * NX
    lane = lax.broadcasted_iota(jnp.int32, (C, 128), 1)
    odd_slot = lane // 32 % 2 == 1
    upper = lane >= 64

    @pl.when(step == 0)
    def _():
        for index, (owner, part, group, k) in enumerate(blocks):
            values = r_ref[owner, part, group, :, CJ * k : CJ * k + CJ].astype(F32)
            for tile in range(4):
                end = min(128 * tile + 128, CJ)
                in_scr[tile, index * modes_here : (index + 1) * modes_here, : end - 128 * tile] = values[
                    :, 128 * tile : end
                ]
        for mode in range(modes_here):
            pair, half = mode // 2, mode % 2
            tiles = [in_scr[tile, pl.ds(mode, cells, stride=modes_here), :] for tile in range(4)]
            block = jnp.concatenate(tiles, axis=1).astype(BF16)
            cols = lax.dot_general(block, gx_ref[...], (((0,), (0,)), ((), ())), preferred_element_type=F32)
            o_scr[half] = cols
            for a in range(6):
                pieces = [o_scr[half, pl.ds(4 * a + r, C, stride=MY), :] for r in range(4)]
                first = jnp.where(odd_slot, pieces[1], pieces[0])
                second = jnp.where(odd_slot, pieces[3], pieces[2])
                lanes = slice(128 * a, 128 * a + 128)
                ut_scr[half, pair, 0, :C, lanes] = jnp.where(upper, pltpu.roll(second, 64, 1), first)
                ut_scr[half, pair, 1, :C, lanes] = jnp.where(upper, second, pltpu.roll(first, 64, 1))
        even = dot32(ut_scr[0].reshape(count * 48, 768).astype(BF16), perm_ref[0])
        odd = dot32(ut_scr[1].reshape(count * 48, 768).astype(BF16), perm_ref[1])
        even = even.reshape(count, 2, 24, 640)
        odd = odd.reshape(count, 2, 24, 640)
        u_scr[:, :, :, :512] = even[:, :, :, :512]
        u_scr[:, :, :, 512:640] = even[:, :, :, 512:] + odd[:, :, :, :128]
        u_scr[:, :, :, 640:] = odd[:, :, :, 128:]

    for sub in range(PAIRS_STEP):
        here = PAIRS_STEP * step + sub
        for part in range(2):
            u_ref[0, part, :, KB * sub : KB * sub + KB] = u_scr[here, part, :C, :].astype(BF16)
        for chunk in range(3):
            lanes = slice(384 * chunk, 384 * chunk + 384)
            w_lanes = slice(KB * sub + 384 * chunk, KB * sub + 384 * chunk + 384)
            if backward:
                real = u_scr[here, 0, :C, lanes]
                imag = u_scr[here, 1, :C, lanes]
                for ch in range(C):
                    w_real = w_ref[0, ch, :, w_lanes].astype(F32)
                    w_imag = w_ref[1, ch, :, w_lanes].astype(F32)
                    v_scr[here, 0, ch : ch + 1, lanes] = jnp.sum(w_real * real + w_imag * imag, axis=0, keepdims=True)
                    v_scr[here, 1, ch : ch + 1, lanes] = jnp.sum(w_real * imag - w_imag * real, axis=0, keepdims=True)
            else:
                real = jnp.zeros((C, 384), F32)
                imag = jnp.zeros((C, 384), F32)
                for ch in range(C):
                    w_real = w_ref[0, ch, :, w_lanes].astype(F32)
                    w_imag = w_ref[1, ch, :, w_lanes].astype(F32)
                    u_real = u_scr[here, 0, ch : ch + 1, lanes]
                    u_imag = u_scr[here, 1, ch : ch + 1, lanes]
                    real = real + w_real * u_real - w_imag * u_imag
                    imag = imag + w_real * u_imag + w_imag * u_real
                v_scr[here, 0, :C, lanes] = real
                v_scr[here, 1, :C, lanes] = imag

    @pl.when(step == steps - 1)
    def _():
        for half in range(2):
            values = v_scr[:, :, :, 512 * half : 512 * half + 640].reshape(count * 48, 640).astype(BF16)
            moved = lax.dot_general(values, perm_ref[half], (((1,), (1,)), ((), ())), preferred_element_type=F32)
            ut_scr[half] = moved.reshape(count, 2, 24, 768)
        o_scr[...] = jnp.zeros_like(o_scr)
        for mode in range(modes_here):
            pair, half = mode // 2, mode % 2
            for a in range(6):
                lanes = slice(128 * a, 128 * a + 128)
                real = ut_scr[half, pair, 0, :C, lanes]
                imag = ut_scr[half, pair, 1, :C, lanes]
                first = jnp.where(upper, pltpu.roll(imag, 64, 1), real)
                second = jnp.where(upper, imag, pltpu.roll(real, 64, 1))
                for r, values in enumerate((first, first, second, second)):
                    kept = odd_slot if r % 2 else jnp.logical_not(odd_slot)
                    o_scr[half, pl.ds(4 * a + r, C, stride=MY), :] = jnp.where(kept, values, 0.0)
            back = lax.dot_general(
                gx_ref[...], o_scr[half].astype(BF16), (((1,), (1,)), ((), ())), preferred_element_type=F32
            )
            for tile in range(4):
                out_scr[tile, pl.ds(mode, cells, stride=modes_here), :] = back[:, 128 * tile : 128 * tile + 128]
        for index, (owner, part, group, k) in enumerate(blocks):
            rows = slice(index * modes_here, (index + 1) * modes_here)
            values = jnp.concatenate([out_scr[tile, rows, :] for tile in range(4)], axis=1)
            q_ref[owner, part, group, :, CJ * k : CJ * k + CJ] = values[:, :CJ].astype(BF16)


def weight_kernel(*refs):
    out_ref = refs[-1]
    pieces = refs[:-1]
    width = out_ref.shape[3]
    lane_step = 384 if width % 384 == 0 else width
    row = pl.ds(pl.program_id(0), 1)
    for first in range(0, width, lane_step):
        lanes = slice(first, first + lane_step)
        real = jnp.zeros((C, lane_step), F32)
        imag = jnp.zeros((C, lane_step), F32)
        for u_ref, g_ref in zip(pieces[::2], pieces[1::2]):
            u_real = u_ref[0, row, lanes]
            u_imag = u_ref[1, row, lanes]
            g_real = g_ref[0, :, lanes].astype(F32)
            g_imag = g_ref[1, :, lanes].astype(F32)
            real = real + u_real * g_real + u_imag * g_imag
            imag = imag + u_real * g_imag - u_imag * g_real
        out_ref[0, 0, :, lanes] = real
        out_ref[1, 0, :, lanes] = imag


def cost(micros):
    return pl.CostEstimate(flops=int(micros * 1e9), transcendentals=0, bytes_accessed=int(micros * 3e6))


def whole(_):
    return pl.BlockSpec(memory_space=pltpu.VMEM)


def fixed(array):
    zeros = (0,) * len(array.shape)
    return pl.BlockSpec(array.shape, lambda i: zeros)


def params(mebibytes=52):
    return pltpu.CompilerParams(dimension_semantics=("arbitrary",), vmem_limit_bytes=mebibytes * MIB)


def shape_of(shape, kind):
    return jax.ShapeDtypeStruct(shape, kind)


def local(signal, cotangent, spec_weight, point_weight, bias):
    samples, depth_len, x_rows, merged = signal.shape
    owners = NX // x_rows
    modes_here = MZT // owners
    modes = modes_here * KM
    dp_size = lax.axis_size("dp")
    share = modes // dp_size
    rows_all = ZT * x_rows
    depth_rows = 128
    block = depth_rows * x_rows
    steps = ZT // depth_rows

    forward_np, inverse_np = depth_tables()
    yf_np, yi_np, yi_half_np = y_tiles()
    zf_fwd, zf_inv = jnp.asarray(forward_np), jnp.asarray(inverse_np)
    zi_fwd, zi_inv = jnp.asarray(forward_np.T.reshape(2, ZT, -1)), jnp.asarray(inverse_np.T.reshape(2, ZT, -1))
    yf, yi, yi_half = jnp.asarray(yf_np), jnp.asarray(yi_np), jnp.asarray(yi_half_np)
    perm = jnp.asarray(lane_perms())
    gx = jnp.asarray(x_table(x_rows))
    spread = jnp.asarray((np.arange(CY)[:, None] // NY == np.arange(C)[None, :]).astype(BF))
    same_y = jnp.asarray(np.arange(NY)[:, None] == np.arange(NY)[None, :])

    sig = signal.reshape(rows_all, CY)
    cot = cotangent.reshape(rows_all, CY)
    joined = math.gcd(x_rows, 4)
    payload = shape_of((owners, 2, x_rows // joined, modes_here, joined * CJ), BF16)
    payload_spec = pl.BlockSpec(payload.shape, lambda i: (0, 0, 0, 0, 0))
    zi_spec = pl.BlockSpec((2, depth_rows, 2 * MZT), lambda i: (0, i, 0))
    row_spec = pl.BlockSpec((block, CY), lambda i: (i, 0))
    y_scr = pltpu.VMEM((8, block, 128), F32)
    yt_scr = pltpu.VMEM((x_rows, 2 * ZT, LANES), BF16)
    z_scr = pltpu.VMEM((8, block, 128), F32)
    sizes = dict(x_rows=x_rows, depth_rows=depth_rows)

    def point_block(weights):
        wide = dot32(dot32(spread, weights).astype(BF16), spread.T)
        row_y = lax.broadcasted_iota(jnp.int32, (CY, CY), 0) % NY
        col_y = lax.broadcasted_iota(jnp.int32, (CY, CY), 1) % NY
        return jnp.where(row_y == col_y, wide, 0.0).astype(BF16)

    def point(kernel, values, weights, *rest):
        matrix = point_block(weights)
        return pl.pallas_call(
            kernel,
            grid=(steps,),
            in_specs=[row_spec, whole(matrix)] + [whole(array) for array in rest],
            out_specs=row_spec,
            out_shape=shape_of((rows_all, CY), BF16),
            compiler_params=params(), cost_estimate=cost(18),
            name="point",
        )(values, matrix, *rest)

    width = PAIRS_STEP * KB
    aligned = share % width == 0

    def modes_call(received, backward):
        pairs = modes_here // 2
        if aligned:
            per = share // width
            u_shape = shape_of((dp_size, 2, C, share), BF16)
            u_spec = pl.BlockSpec((1, 2, C, width), lambda i: (i // per, 0, 0, i % per))
        else:
            u_shape = shape_of((1, 2, C, modes), BF16)
            u_spec = pl.BlockSpec((1, 2, C, width), lambda i: (0, 0, 0, i))
        return pl.pallas_call(
            functools.partial(mode_kernel, backward=backward),
            grid=(pairs // PAIRS_STEP,),
            in_specs=[
                whole(received),
                pl.BlockSpec((2, C, C, width), lambda i: (0, 0, 0, i)),
                whole(gx),
                whole(perm),
            ],
            out_specs=(u_spec, payload_spec),
            out_shape=(u_shape, payload),
            scratch_shapes=[
                pltpu.VMEM((4, 2 * NX * modes_here, 128), F32),
                pltpu.VMEM((4, 2 * NX * modes_here, 128), F32),
                pltpu.VMEM((2, LANES, 128), F32),
                pltpu.VMEM((2, pairs, 2, 24, 768), F32),
                pltpu.VMEM((pairs, 2, 24, KB), F32),
                pltpu.VMEM((pairs, 2, 24, KB), F32),
            ],
            compiler_params=params(46), cost_estimate=cost(27),
            name="modes",
        )(received, spec_weight, gx, perm)

    def exchange(values):
        return lax.all_to_all(values, "space", split_axis=0, concat_axis=0, tiled=True)

    me = lax.axis_index("dp")

    def to_owners(spectrum):
        if aligned:
            cut = spectrum
        else:
            cut = jnp.transpose(spectrum[0].reshape(2, C, dp_size, share), (2, 0, 1, 3))
        pieces = []
        for shift in range(dp_size):
            piece = lax.dynamic_index_in_dim(cut, (me + shift) % dp_size, 0, keepdims=False)
            if shift:
                piece = lax.ppermute(piece, "dp", [(i, (i + shift) % dp_size) for i in range(dp_size)])
            pieces.append(piece)
        return pieces

    coeffs = pl.pallas_call(
        functools.partial(analyse_kernel, **sizes),
        grid=(steps,),
        in_specs=[row_spec, fixed(yf), fixed(zf_fwd)],
        out_specs=payload_spec,
        out_shape=payload,
        scratch_shapes=[y_scr, yt_scr],
        compiler_params=params(), cost_estimate=cost(14),
        name="analyse",
    )(sig, yf, zf_fwd)
    bias_row = jnp.repeat(bias.astype(F32), NY).reshape(1, CY)
    direct = point(direct_kernel, sig, point_weight, bias_row)
    received, direct = lax.optimization_barrier((exchange(coeffs), direct))
    u_hat, v_cells = modes_call(received, False)
    u_pieces = [piece.astype(F32) for piece in to_owners(u_hat)]
    v_here, u_pieces = lax.optimization_barrier((exchange(v_cells), u_pieces))
    hidden, e_coeffs = pl.pallas_call(
        functools.partial(middle_kernel, **sizes),
        grid=(steps,),
        in_specs=[
            whole(payload), row_spec, row_spec, zi_spec, whole(yi_half), whole(yf), fixed(zf_inv),
        ],
        out_specs=(row_spec, payload_spec),
        out_shape=(shape_of((rows_all, CY), BF16), payload),
        scratch_shapes=[z_scr, y_scr, yt_scr],
        compiler_params=params(), cost_estimate=cost(32),
        name="middle",
    )(v_here, direct, cot, zi_inv, yi_half, yf, zf_inv)
    pointwise = point(point_kernel, hidden, point_weight.T)
    received, pointwise = lax.optimization_barrier((exchange(e_coeffs), pointwise))
    g_hat, d_cells = modes_call(received, True)
    d_here = exchange(d_cells)
    grad_signal = pl.pallas_call(
        functools.partial(final_kernel, x_rows=x_rows),
        grid=(steps,),
        in_specs=[whole(payload), row_spec, zi_spec, whole(yi)],
        out_specs=row_spec,
        out_shape=shape_of((rows_all, CY), BF16),
        scratch_shapes=[z_scr],
        compiler_params=params(), cost_estimate=cost(16),
        name="final",
    )(d_here, pointwise, zi_fwd, yi)
    pieces = [piece for pair in zip(u_pieces, to_owners(g_hat)) for piece in pair]
    spec_grad = pl.pallas_call(
        weight_kernel,
        grid=(C,),
        in_specs=[whole(piece) for piece in pieces],
        out_specs=pl.BlockSpec((2, 1, C, share), lambda i: (0, i, 0, 0)),
        out_shape=shape_of((2, C, C, share), F32),
        compiler_params=params(), cost_estimate=cost(13),
        name="weight",
    )(*pieces)
    return (grad_signal.reshape(signal.shape), spec_grad)


def solution(mesh):
    return jax.shard_map(
        local,
        mesh=mesh,
        in_specs=(
            P("dp", None, "space", None),
            P("dp", None, "space", None),
            P(None, None, None, "space"),
            P(),
            P(),
        ),
        out_specs=(P("dp", None, "space", None), P(None, None, None, ("space", "dp"))),
        check_vma=False,
    )
```

```python
import functools
import math

import jax
import jax.numpy as jnp
import ml_dtypes
import numpy as np
from jax import lax
from jax.experimental import pallas as pl
from jax.experimental.pallas import tpu as pltpu
from jax.sharding import PartitionSpec as P

NX = 64
NY = 64
NZ = 32
NT = 16
ZT = NZ * NT
C = 20
MX = 24
MY = 24
MZ = 16
MT = 8
MZT = 128
CY = C * NY
LANES = 512
CJ = C * MY
KM = MX * MY
KB = 2 * KM
PAIRS_STEP = 2
BF = ml_dtypes.bfloat16
BF16 = jnp.bfloat16
F32 = jnp.float32
MIB = 1024 * 1024
PAIRS = ((0, 0), (0, 1), (1, 1), (1, 2), (2, 2), (2, 3), (3, 4))


def retained(mode_count, length):
    positions = np.arange(mode_count)
    return np.where(positions < mode_count // 2, positions, length - mode_count + positions)


def complex_table(mode_count, length):
    freqs = retained(mode_count, length)
    turns = freqs[:, None] * np.arange(length)[None, :] % length
    angles = turns * (2.0 * math.pi / length)
    norm_scale = 1.0 / math.sqrt(length)
    cos_part = np.cos(angles) * norm_scale
    sin_part = np.sin(angles) * norm_scale
    upper_rows = np.stack([cos_part, sin_part], axis=1)
    lower_rows = np.stack([-sin_part, cos_part], axis=1)
    return np.stack([upper_rows, lower_rows], axis=0)


def depth_tables():
    depth_freq = retained(MZ, NZ)
    time_freq = np.arange(MT)
    depth_turns = depth_freq[:, None] * np.arange(NZ)[None, :] % NZ
    time_turns = time_freq[:, None] * np.arange(NT)[None, :] % NT
    turns = depth_turns[:, None, :, None] * NT + time_turns[None, :, None, :] * NZ
    angles = turns * (2.0 * math.pi / ZT)
    norm_scale = 1.0 / math.sqrt(ZT)
    forward = np.stack([np.cos(angles), -np.sin(angles)], axis=2) * norm_scale
    doubling = np.where(time_freq == 0, 1.0, 2.0)
    inverse = forward * doubling[None, :, None, None, None]

    def square(table):
        real, imag = table.reshape(MZT, 2, ZT).transpose(1, 0, 2)
        return np.block([[real, -imag], [imag, real]]).astype(BF)

    return square(forward), square(inverse)


def y_tiles():
    table = complex_table(MY, NY)
    full = np.zeros((2, CY, LANES))
    for ch in range(C):
        full[:, ch * NY : (ch + 1) * NY, ch * MY : (ch + 1) * MY] = table[:, :, 0, :].transpose(0, 2, 1)
    tiles = []
    for tile, group in PAIRS:
        rows = full[:, 256 * group : 256 * group + 256, 128 * tile : 128 * tile + 128]
        tiles.append(np.concatenate([rows[0], rows[1]], axis=1))
    tiles = np.stack(tiles)
    back = tiles.transpose(0, 2, 1)
    return tiles.astype(BF), back.astype(BF), (back * math.sqrt(0.5)).astype(BF)


def x_table(x_rows):
    table = complex_table(MX, NX)
    split = table.reshape(2, MX, 2, NX // x_rows, x_rows).transpose(3, 2, 4, 0, 1)
    out = np.zeros((NX // x_rows, 2, x_rows, 2, 2, 32))
    out[..., :MX] = split[:, :, :, :, None, :]
    return out.reshape(2 * NX, 128).astype(BF)


def lane_perm():
    perm = np.zeros((768, 640))
    for i in range(MX):
        for j in range(MY):
            perm[128 * (j // 4) + 32 * (j % 4) + i, i * MY + j] = 1.0
    return perm.astype(BF)


def dot32(left, right):
    return jnp.dot(left, right, preferred_element_type=F32)


def forward_y(rows, yf_ref, y_scr):
    for tile in range(4):
        total = None
        for k, (pair_tile, group) in enumerate(PAIRS):
            if pair_tile == tile:
                part = dot32(rows[:, 256 * group : 256 * group + 256], yf_ref[k])
                total = part if total is None else total + part
        y_scr[2 * tile] = total[:, :128]
        y_scr[2 * tile + 1] = total[:, 128:]


def spread_x(y_scr, yt_scr, step, x_rows, depth_rows):
    start = pl.multiple_of(step * depth_rows, depth_rows)
    for x in range(x_rows):
        for tile in range(4):
            for part in range(2):
                piece = y_scr[2 * tile + part, pl.ds(x, depth_rows, stride=x_rows), :].astype(BF16)
                yt_scr[x, pl.ds(part * ZT + start, depth_rows), 128 * tile : 128 * tile + 128] = piece


def forward_depth(zf_ref, yt_scr, out_ref, x_rows):
    owners, _, x_groups, modes_here, _ = out_ref.shape
    joined = x_rows // x_groups
    for x in range(x_rows):
        coeffs = dot32(zf_ref[...], yt_scr[x]).astype(BF16)
        lane = CJ * (x % joined)
        for owner in range(owners):
            for part in range(2):
                row = part * MZT + owner * modes_here
                out_ref[owner, part, x // joined, :, lane : lane + CJ] = coeffs[row : row + modes_here, :CJ]


def inverse_depth(q_ref, zi_ref, z_scr, x_rows):
    owners, _, x_groups, _, _ = q_ref.shape
    joined = x_rows // x_groups
    depth_rows = zi_ref.shape[1]
    margin = jnp.zeros((2 * MZT, LANES - CJ), BF16)
    table = jnp.concatenate([zi_ref[0], zi_ref[1]], axis=0)
    for x in range(x_rows):
        group, lanes = x // joined, slice(CJ * (x % joined), CJ * (x % joined) + CJ)
        rows = [q_ref[owner, part, group, :, lanes] for part in range(2) for owner in range(owners)]
        rows = jnp.concatenate([jnp.concatenate(rows, axis=0), margin], axis=1)
        grid_rows = dot32(table, rows)
        for part in range(2):
            for tile in range(4):
                z_scr[2 * tile + part, pl.ds(x, depth_rows, stride=x_rows), :] = grid_rows[
                    part * depth_rows : (part + 1) * depth_rows, 128 * tile : 128 * tile + 128
                ]


def inverse_y(z_scr, yi_ref, group):
    total = None
    for k, (tile, pair_group) in enumerate(PAIRS):
        if pair_group == group:
            rows = jnp.concatenate([z_scr[2 * tile], z_scr[2 * tile + 1]], axis=1)
            part = dot32(rows.astype(BF16), yi_ref[k])
            total = part if total is None else total + part
    return total


def twice_slope(scaled):
    gauss = jnp.exp2(scaled * scaled * -math.log2(math.e))
    return (1.0 + lax.erf(scaled)) + (2.0 / math.sqrt(math.pi)) * scaled * gauss


def analyse_kernel(s_ref, yf_ref, zf_ref, out_ref, y_scr, yt_scr, *, x_rows, depth_rows):
    step = pl.program_id(0)
    forward_y(s_ref[...], yf_ref, y_scr)
    spread_x(y_scr, yt_scr, step, x_rows, depth_rows)

    @pl.when(step == pl.num_programs(0) - 1)
    def _():
        forward_depth(zf_ref, yt_scr, out_ref, x_rows)


def middle_kernel(
    q_ref, d_ref, cot_ref, zi_ref, yi_ref, yf_ref, zf_ref, h_ref, out_ref,
    z_scr, y_scr, yt_scr, *, x_rows, depth_rows,
):
    step = pl.program_id(0)
    block = x_rows * depth_rows

    inverse_depth(q_ref, zi_ref, z_scr, x_rows)
    for group in range(5):
        lanes = slice(256 * group, 256 * group + 256)
        total = inverse_y(z_scr, yi_ref, group)
        for first in range(0, block, 64):
            rows = slice(first, first + 64)
            scaled = total[rows] + d_ref[rows, lanes].astype(F32)
            twice_hidden = cot_ref[rows, lanes].astype(F32) * twice_slope(scaled)
            h_ref[rows, lanes] = twice_hidden.astype(BF16)
    forward_y(h_ref[...], yf_ref, y_scr)
    spread_x(y_scr, yt_scr, step, x_rows, depth_rows)

    @pl.when(step == pl.num_programs(0) - 1)
    def _():
        forward_depth(zf_ref, yt_scr, out_ref, x_rows)


def final_kernel(q_ref, p_ref, zi_ref, yi_ref, out_ref, z_scr, *, x_rows):
    inverse_depth(q_ref, zi_ref, z_scr, x_rows)
    for group in range(5):
        lanes = slice(256 * group, 256 * group + 256)
        total = inverse_y(z_scr, yi_ref, group) + p_ref[:, lanes].astype(F32)
        out_ref[:, lanes] = total.astype(BF16)


def point_kernel(s_ref, b_ref, out_ref):
    out_ref[...] = dot32(s_ref[...], b_ref[...]).astype(BF16)


def direct_kernel(s_ref, b_ref, bias_ref, out_ref):
    out_ref[...] = ((dot32(s_ref[...], b_ref[...]) + bias_ref[...]) * math.sqrt(0.5)).astype(BF16)


def mode_kernel(
    r_ref, w_ref, gx_ref, perm_ref, u_ref, q_ref,
    in_scr, out_scr, o_scr, ut_scr, u_scr, v_scr, *, backward,
):
    step = pl.program_id(0)
    steps = pl.num_programs(0)
    owners, _, x_groups, modes_here, width = r_ref.shape
    joined = width // CJ
    blocks = [(o, p, g, k) for o in range(owners) for p in range(2) for g in range(x_groups) for k in range(joined)]
    count = modes_here // 2
    cells = 2 * NX
    lane = lax.broadcasted_iota(jnp.int32, (C, 128), 1)
    odd_slot = lane // 32 % 2 == 1
    upper = lane >= 64

    @pl.when(step == 0)
    def _():
        for index, (owner, part, group, k) in enumerate(blocks):
            values = r_ref[owner, part, group, :, CJ * k : CJ * k + CJ].astype(F32)
            for tile in range(4):
                end = min(128 * tile + 128, CJ)
                in_scr[tile, index * modes_here : (index + 1) * modes_here, : end - 128 * tile] = values[
                    :, 128 * tile : end
                ]
        for mode in range(modes_here):
            pair, half = mode // 2, mode % 2
            tiles = [in_scr[tile, pl.ds(mode, cells, stride=modes_here), :] for tile in range(4)]
            block = jnp.concatenate(tiles, axis=1).astype(BF16)
            cols = lax.dot_general(block, gx_ref[...], (((0,), (0,)), ((), ())), preferred_element_type=F32)
            o_scr[half] = cols
            for a in range(6):
                pieces = [o_scr[half, pl.ds(4 * a + r, C, stride=MY), :] for r in range(4)]
                first = jnp.where(odd_slot, pieces[1], pieces[0])
                second = jnp.where(odd_slot, pieces[3], pieces[2])
                lanes = slice(128 * a, 128 * a + 128)
                ut_scr[half, pair, 0, :C, lanes] = jnp.where(upper, pltpu.roll(second, 64, 1), first)
                ut_scr[half, pair, 1, :C, lanes] = jnp.where(upper, second, pltpu.roll(first, 64, 1))
        moved = dot32(ut_scr[...].reshape(2 * count * 48, 768).astype(BF16), perm_ref[...])
        even = moved[: count * 48].reshape(count, 2, 24, 640)
        odd = pltpu.roll(moved[count * 48 :], 64, 1).reshape(count, 2, 24, 640)
        u_scr[:, :, :, :512] = even[:, :, :, :512]
        u_scr[:, :, :, 512:640] = even[:, :, :, 512:] + odd[:, :, :, :128]
        u_scr[:, :, :, 640:] = odd[:, :, :, 128:]

    for sub in range(PAIRS_STEP):
        here = PAIRS_STEP * step + sub
        for part in range(2):
            u_ref[0, part, :, KB * sub : KB * sub + KB] = u_scr[here, part, :C, :].astype(BF16)
        for chunk in range(3):
            lanes = slice(384 * chunk, 384 * chunk + 384)
            w_lanes = slice(KB * sub + 384 * chunk, KB * sub + 384 * chunk + 384)
            if backward:
                real = u_scr[here, 0, :C, lanes]
                imag = u_scr[here, 1, :C, lanes]
                for ch in range(C):
                    w_real = w_ref[0, ch, :, w_lanes].astype(F32)
                    w_imag = w_ref[1, ch, :, w_lanes].astype(F32)
                    v_scr[here, 0, ch : ch + 1, lanes] = jnp.sum(w_real * real + w_imag * imag, axis=0, keepdims=True)
                    v_scr[here, 1, ch : ch + 1, lanes] = jnp.sum(w_real * imag - w_imag * real, axis=0, keepdims=True)
            else:
                real = jnp.zeros((C, 384), F32)
                imag = jnp.zeros((C, 384), F32)
                for ch in range(C):
                    w_real = w_ref[0, ch, :, w_lanes].astype(F32)
                    w_imag = w_ref[1, ch, :, w_lanes].astype(F32)
                    u_real = u_scr[here, 0, ch : ch + 1, lanes]
                    u_imag = u_scr[here, 1, ch : ch + 1, lanes]
                    real = real + w_real * u_real - w_imag * u_imag
                    imag = imag + w_real * u_imag + w_imag * u_real
                v_scr[here, 0, :C, lanes] = real
                v_scr[here, 1, :C, lanes] = imag

    @pl.when(step == steps - 1)
    def _():
        even = v_scr[:, :, :, :640].reshape(count * 48, 640)
        odd = pltpu.roll(v_scr[:, :, :, 512:].reshape(count * 48, 640), 576, 1)
        values = jnp.concatenate([even, odd], axis=0).astype(BF16)
        moved = lax.dot_general(values, perm_ref[...], (((1,), (1,)), ((), ())), preferred_element_type=F32)
        ut_scr[...] = moved.reshape(2, count, 2, 24, 768)
        o_scr[...] = jnp.zeros_like(o_scr)
        for mode in range(modes_here):
            pair, half = mode // 2, mode % 2
            for a in range(6):
                lanes = slice(128 * a, 128 * a + 128)
                real = ut_scr[half, pair, 0, :C, lanes]
                imag = ut_scr[half, pair, 1, :C, lanes]
                first = jnp.where(upper, pltpu.roll(imag, 64, 1), real)
                second = jnp.where(upper, imag, pltpu.roll(real, 64, 1))
                for r, values in enumerate((first, first, second, second)):
                    kept = odd_slot if r % 2 else jnp.logical_not(odd_slot)
                    o_scr[half, pl.ds(4 * a + r, C, stride=MY), :] = jnp.where(kept, values, 0.0)
            back = lax.dot_general(
                gx_ref[...], o_scr[half].astype(BF16), (((1,), (1,)), ((), ())), preferred_element_type=F32
            )
            for tile in range(4):
                out_scr[tile, pl.ds(mode, cells, stride=modes_here), :] = back[:, 128 * tile : 128 * tile + 128]
        for index, (owner, part, group, k) in enumerate(blocks):
            rows = slice(index * modes_here, (index + 1) * modes_here)
            values = jnp.concatenate([out_scr[tile, rows, :] for tile in range(4)], axis=1)
            q_ref[owner, part, group, :, CJ * k : CJ * k + CJ] = values[:, :CJ].astype(BF16)


def weight_kernel(*refs):
    out_ref = refs[-1]
    pieces = refs[:-1]
    width = out_ref.shape[3]
    lane_step = 384 if width % 384 == 0 else width
    row = pl.ds(pl.program_id(0), 1)
    for first in range(0, width, lane_step):
        lanes = slice(first, first + lane_step)
        real = jnp.zeros((C, lane_step), F32)
        imag = jnp.zeros((C, lane_step), F32)
        for u_ref, g_ref in zip(pieces[::2], pieces[1::2]):
            u_real = u_ref[0, row, lanes]
            u_imag = u_ref[1, row, lanes]
            g_real = g_ref[0, :, lanes].astype(F32)
            g_imag = g_ref[1, :, lanes].astype(F32)
            real = real + u_real * g_real + u_imag * g_imag
            imag = imag + u_real * g_imag - u_imag * g_real
        out_ref[0, 0, :, lanes] = real
        out_ref[1, 0, :, lanes] = imag


def cost(micros):
    return pl.CostEstimate(flops=int(micros * 1e9), transcendentals=0, bytes_accessed=int(micros * 3e6))


def whole(_):
    return pl.BlockSpec(memory_space=pltpu.VMEM)


def fixed(array):
    zeros = (0,) * len(array.shape)
    return pl.BlockSpec(array.shape, lambda i: zeros)


def params(mebibytes=52):
    return pltpu.CompilerParams(dimension_semantics=("arbitrary",), vmem_limit_bytes=mebibytes * MIB)


def shape_of(shape, kind):
    return jax.ShapeDtypeStruct(shape, kind)


def local(signal, cotangent, spec_weight, point_weight, bias):
    samples, depth_len, x_rows, merged = signal.shape
    owners = NX // x_rows
    modes_here = MZT // owners
    modes = modes_here * KM
    dp_size = lax.axis_size("dp")
    share = modes // dp_size
    rows_all = ZT * x_rows
    depth_rows = 128
    block = depth_rows * x_rows
    steps = ZT // depth_rows

    forward_np, inverse_np = depth_tables()
    yf_np, yi_np, yi_half_np = y_tiles()
    zf_fwd, zf_inv = jnp.asarray(forward_np), jnp.asarray(inverse_np)
    zi_fwd, zi_inv = jnp.asarray(forward_np.T.reshape(2, ZT, -1)), jnp.asarray(inverse_np.T.reshape(2, ZT, -1))
    yf, yi, yi_half = jnp.asarray(yf_np), jnp.asarray(yi_np), jnp.asarray(yi_half_np)
    yf_half = jnp.asarray((yf_np.astype(np.float32) * 0.5).astype(BF))
    perm = jnp.asarray(lane_perm())
    gx = jnp.asarray(x_table(x_rows))
    spread = jnp.asarray((np.arange(CY)[:, None] // NY == np.arange(C)[None, :]).astype(BF))
    same_y = jnp.asarray(np.arange(NY)[:, None] == np.arange(NY)[None, :])

    sig = signal.reshape(rows_all, CY)
    cot = cotangent.reshape(rows_all, CY)
    joined = math.gcd(x_rows, 4)
    payload = shape_of((owners, 2, x_rows // joined, modes_here, joined * CJ), BF16)
    payload_spec = pl.BlockSpec(payload.shape, lambda i: (0, 0, 0, 0, 0))
    zi_spec = pl.BlockSpec((2, depth_rows, 2 * MZT), lambda i: (0, i, 0))
    row_spec = pl.BlockSpec((block, CY), lambda i: (i, 0))
    y_scr = pltpu.VMEM((8, block, 128), F32)
    yt_scr = pltpu.VMEM((x_rows, 2 * ZT, LANES), BF16)
    z_scr = pltpu.VMEM((8, block, 128), F32)
    sizes = dict(x_rows=x_rows, depth_rows=depth_rows)

    def point_block(weights):
        wide = dot32(dot32(spread, weights).astype(BF16), spread.T)
        row_y = lax.broadcasted_iota(jnp.int32, (CY, CY), 0) % NY
        col_y = lax.broadcasted_iota(jnp.int32, (CY, CY), 1) % NY
        return jnp.where(row_y == col_y, wide, 0.0).astype(BF16)

    def point(kernel, values, weights, *rest):
        matrix = point_block(weights)
        return pl.pallas_call(
            kernel,
            grid=(steps,),
            in_specs=[row_spec, whole(matrix)] + [whole(array) for array in rest],
            out_specs=row_spec,
            out_shape=shape_of((rows_all, CY), BF16),
            compiler_params=params(), cost_estimate=cost(18),
            name="point",
        )(values, matrix, *rest)

    width = PAIRS_STEP * KB
    aligned = share % width == 0

    def modes_call(received, backward):
        pairs = modes_here // 2
        if aligned:
            per = share // width
            u_shape = shape_of((dp_size, 2, C, share), BF16)
            u_spec = pl.BlockSpec((1, 2, C, width), lambda i: (i // per, 0, 0, i % per))
        else:
            u_shape = shape_of((1, 2, C, modes), BF16)
            u_spec = pl.BlockSpec((1, 2, C, width), lambda i: (0, 0, 0, i))
        return pl.pallas_call(
            functools.partial(mode_kernel, backward=backward),
            grid=(pairs // PAIRS_STEP,),
            in_specs=[
                whole(received),
                pl.BlockSpec((2, C, C, width), lambda i: (0, 0, 0, i)),
                whole(gx),
                whole(perm),
            ],
            out_specs=(u_spec, payload_spec),
            out_shape=(u_shape, payload),
            scratch_shapes=[
                pltpu.VMEM((4, 2 * NX * modes_here, 128), F32),
                pltpu.VMEM((4, 2 * NX * modes_here, 128), F32),
                pltpu.VMEM((2, LANES, 128), F32),
                pltpu.VMEM((2, pairs, 2, 24, 768), F32),
                pltpu.VMEM((pairs, 2, 24, KB), F32),
                pltpu.VMEM((pairs, 2, 24, KB), F32),
            ],
            compiler_params=params(46), cost_estimate=cost(27),
            name="modes",
        )(received, spec_weight, gx, perm)

    def exchange(values):
        return lax.all_to_all(values, "space", split_axis=0, concat_axis=0, tiled=True)

    me = lax.axis_index("dp")

    def to_owners(spectrum):
        if aligned:
            cut = spectrum
        else:
            cut = jnp.transpose(spectrum[0].reshape(2, C, dp_size, share), (2, 0, 1, 3))
        pieces = []
        for shift in range(dp_size):
            piece = lax.dynamic_index_in_dim(cut, (me + shift) % dp_size, 0, keepdims=False)
            if shift:
                piece = lax.ppermute(piece, "dp", [(i, (i + shift) % dp_size) for i in range(dp_size)])
            pieces.append(piece)
        return pieces

    coeffs = pl.pallas_call(
        functools.partial(analyse_kernel, **sizes),
        grid=(steps,),
        in_specs=[row_spec, fixed(yf), fixed(zf_fwd)],
        out_specs=payload_spec,
        out_shape=payload,
        scratch_shapes=[y_scr, yt_scr],
        compiler_params=params(), cost_estimate=cost(14),
        name="analyse",
    )(sig, yf, zf_fwd)
    bias_row = jnp.repeat(bias.astype(F32), NY).reshape(1, CY)
    direct = point(direct_kernel, sig, point_weight, bias_row)
    received, direct = lax.optimization_barrier((exchange(coeffs), direct))
    u_hat, v_cells = modes_call(received, False)
    u_pieces = [piece.astype(F32) for piece in to_owners(u_hat)]
    v_here, u_pieces = lax.optimization_barrier((exchange(v_cells), u_pieces))
    twice_hidden, e_coeffs = pl.pallas_call(
        functools.partial(middle_kernel, **sizes),
        grid=(steps,),
        in_specs=[
            whole(payload), row_spec, row_spec, zi_spec, whole(yi_half), whole(yf_half), fixed(zf_inv),
        ],
        out_specs=(row_spec, payload_spec),
        out_shape=(shape_of((rows_all, CY), BF16), payload),
        scratch_shapes=[z_scr, y_scr, yt_scr],
        compiler_params=params(), cost_estimate=cost(32),
        name="middle",
    )(v_here, direct, cot, zi_inv, yi_half, yf_half, zf_inv)
    pointwise = point(point_kernel, twice_hidden, point_weight.T * 0.5)
    received, pointwise = lax.optimization_barrier((exchange(e_coeffs), pointwise))
    g_hat, d_cells = modes_call(received, True)
    d_here = exchange(d_cells)
    grad_signal = pl.pallas_call(
        functools.partial(final_kernel, x_rows=x_rows),
        grid=(steps,),
        in_specs=[whole(payload), row_spec, zi_spec, whole(yi)],
        out_specs=row_spec,
        out_shape=shape_of((rows_all, CY), BF16),
        scratch_shapes=[z_scr],
        compiler_params=params(), cost_estimate=cost(16),
        name="final",
    )(d_here, pointwise, zi_fwd, yi)
    pieces = [piece for pair in zip(u_pieces, to_owners(g_hat)) for piece in pair]
    spec_grad = pl.pallas_call(
        weight_kernel,
        grid=(C,),
        in_specs=[whole(piece) for piece in pieces],
        out_specs=pl.BlockSpec((2, 1, C, share), lambda i: (0, i, 0, 0)),
        out_shape=shape_of((2, C, C, share), F32),
        compiler_params=params(), cost_estimate=cost(13),
        name="weight",
    )(*pieces)
    return (grad_signal.reshape(signal.shape), spec_grad)


def solution(mesh):
    return jax.shard_map(
        local,
        mesh=mesh,
        in_specs=(
            P("dp", None, "space", None),
            P("dp", None, "space", None),
            P(None, None, None, "space"),
            P(),
            P(),
        ),
        out_specs=(P("dp", None, "space", None), P(None, None, None, ("space", "dp"))),
        check_vma=False,
    )
```

```python
import functools
import math

import jax
import jax.numpy as jnp
import ml_dtypes
import numpy as np
from jax import lax
from jax.experimental import pallas as pl
from jax.experimental.pallas import tpu as pltpu
from jax.sharding import PartitionSpec as P

NX = 64
NY = 64
NZ = 32
NT = 16
ZT = NZ * NT
C = 20
MX = 24
MY = 24
MZ = 16
MT = 8
MZT = 128
CY = C * NY
LANES = 512
CJ = C * MY
KM = MX * MY
KB = 2 * KM
PAIRS_STEP = 2
BF = ml_dtypes.bfloat16
BF16 = jnp.bfloat16
F32 = jnp.float32
MIB = 1024 * 1024
PAIRS = ((0, 0), (0, 1), (1, 1), (1, 2), (2, 2), (2, 3), (3, 4))


def retained(mode_count, length):
    positions = np.arange(mode_count)
    return np.where(positions < mode_count // 2, positions, length - mode_count + positions)


def complex_table(mode_count, length):
    freqs = retained(mode_count, length)
    turns = freqs[:, None] * np.arange(length)[None, :] % length
    angles = turns * (2.0 * math.pi / length)
    norm_scale = 1.0 / math.sqrt(length)
    cos_part = np.cos(angles) * norm_scale
    sin_part = np.sin(angles) * norm_scale
    upper_rows = np.stack([cos_part, sin_part], axis=1)
    lower_rows = np.stack([-sin_part, cos_part], axis=1)
    return np.stack([upper_rows, lower_rows], axis=0)


def depth_tables():
    depth_freq = retained(MZ, NZ)
    time_freq = np.arange(MT)
    depth_turns = depth_freq[:, None] * np.arange(NZ)[None, :] % NZ
    time_turns = time_freq[:, None] * np.arange(NT)[None, :] % NT
    turns = depth_turns[:, None, :, None] * NT + time_turns[None, :, None, :] * NZ
    angles = turns * (2.0 * math.pi / ZT)
    norm_scale = 1.0 / math.sqrt(ZT)
    forward = np.stack([np.cos(angles), -np.sin(angles)], axis=2) * norm_scale
    doubling = np.where(time_freq == 0, 1.0, 2.0)
    inverse = forward * doubling[None, :, None, None, None]

    def square(table):
        real, imag = table.reshape(MZT, 2, ZT).transpose(1, 0, 2)
        return np.block([[real, -imag], [imag, real]]).astype(BF)

    return square(forward), square(inverse)


def y_tiles():
    table = complex_table(MY, NY)
    full = np.zeros((2, CY, LANES))
    for ch in range(C):
        full[:, ch * NY : (ch + 1) * NY, ch * MY : (ch + 1) * MY] = table[:, :, 0, :].transpose(0, 2, 1)
    tiles = []
    for tile, group in PAIRS:
        rows = full[:, 256 * group : 256 * group + 256, 128 * tile : 128 * tile + 128]
        tiles.append(np.concatenate([rows[0], rows[1]], axis=1))
    tiles = np.stack(tiles)
    back = tiles.transpose(0, 2, 1)
    return tiles.astype(BF), back.astype(BF), (back * math.sqrt(0.5)).astype(BF)


def x_table(x_rows):
    table = complex_table(MX, NX)
    split = table.reshape(2, MX, 2, NX // x_rows, x_rows).transpose(3, 2, 4, 0, 1)
    out = np.zeros((NX // x_rows, 2, x_rows, 2, 2, 32))
    out[..., :MX] = split[:, :, :, :, None, :]
    return out.reshape(2 * NX, 128).astype(BF)


def lane_perm():
    perm = np.zeros((768, 640))
    for i in range(MX):
        for j in range(MY):
            perm[128 * (j // 4) + 32 * (j % 4) + i, i * MY + j] = 1.0
    return perm.astype(BF)


def dot32(left, right):
    return jnp.dot(left, right, preferred_element_type=F32)


def forward_y(rows, yf_ref, y_scr):
    for tile in range(4):
        total = None
        for k, (pair_tile, group) in enumerate(PAIRS):
            if pair_tile == tile:
                part = dot32(rows[:, 256 * group : 256 * group + 256], yf_ref[k])
                total = part if total is None else total + part
        y_scr[2 * tile] = total[:, :128]
        y_scr[2 * tile + 1] = total[:, 128:]


def spread_x(y_scr, yt_scr, step, x_rows, depth_rows):
    start = pl.multiple_of(step * depth_rows, depth_rows)
    for x in range(x_rows):
        for tile in range(4):
            for part in range(2):
                piece = y_scr[2 * tile + part, pl.ds(x, depth_rows, stride=x_rows), :].astype(BF16)
                yt_scr[x, pl.ds(part * ZT + start, depth_rows), 128 * tile : 128 * tile + 128] = piece


def forward_depth(zf_ref, yt_scr, out_ref, x_rows):
    owners, _, x_groups, modes_here, _ = out_ref.shape
    joined = x_rows // x_groups
    for x in range(x_rows):
        coeffs = dot32(zf_ref[...], yt_scr[x]).astype(BF16)
        lane = CJ * (x % joined)
        for owner in range(owners):
            for part in range(2):
                row = part * MZT + owner * modes_here
                out_ref[owner, part, x // joined, :, lane : lane + CJ] = coeffs[row : row + modes_here, :CJ]


def inverse_depth(q_ref, zi_ref, z_scr, x_rows):
    owners, _, x_groups, _, _ = q_ref.shape
    joined = x_rows // x_groups
    depth_rows = zi_ref.shape[1]
    margin = jnp.zeros((2 * MZT, LANES - CJ), BF16)
    table = jnp.concatenate([zi_ref[0], zi_ref[1]], axis=0)
    for x in range(x_rows):
        group, lanes = x // joined, slice(CJ * (x % joined), CJ * (x % joined) + CJ)
        rows = [q_ref[owner, part, group, :, lanes] for part in range(2) for owner in range(owners)]
        rows = jnp.concatenate([jnp.concatenate(rows, axis=0), margin], axis=1)
        grid_rows = dot32(table, rows)
        for part in range(2):
            for tile in range(4):
                z_scr[2 * tile + part, pl.ds(x, depth_rows, stride=x_rows), :] = grid_rows[
                    part * depth_rows : (part + 1) * depth_rows, 128 * tile : 128 * tile + 128
                ]


def inverse_y(z_scr, yi_ref, group):
    total = None
    for k, (tile, pair_group) in enumerate(PAIRS):
        if pair_group == group:
            rows = jnp.concatenate([z_scr[2 * tile], z_scr[2 * tile + 1]], axis=1)
            part = dot32(rows.astype(BF16), yi_ref[k])
            total = part if total is None else total + part
    return total


def twice_slope(scaled):
    gauss = jnp.exp2(scaled * scaled * -math.log2(math.e))
    return (1.0 + lax.erf(scaled)) + (2.0 / math.sqrt(math.pi)) * scaled * gauss


def analyse_kernel(s_ref, yf_ref, zf_ref, out_ref, y_scr, yt_scr, *, x_rows, depth_rows):
    step = pl.program_id(0)
    forward_y(s_ref[...], yf_ref, y_scr)
    spread_x(y_scr, yt_scr, step, x_rows, depth_rows)

    @pl.when(step == pl.num_programs(0) - 1)
    def _():
        forward_depth(zf_ref, yt_scr, out_ref, x_rows)


def middle_kernel(
    q_ref, d_ref, cot_ref, zi_ref, yi_ref, yf_ref, zf_ref, h_ref, out_ref,
    z_scr, y_scr, yt_scr, *, x_rows, depth_rows,
):
    step = pl.program_id(0)
    block = x_rows * depth_rows

    inverse_depth(q_ref, zi_ref, z_scr, x_rows)
    for group in range(5):
        lanes = slice(256 * group, 256 * group + 256)
        total = inverse_y(z_scr, yi_ref, group)
        for first in range(0, block, 64):
            rows = slice(first, first + 64)
            scaled = total[rows] + d_ref[rows, lanes].astype(F32)
            twice_hidden = cot_ref[rows, lanes].astype(F32) * twice_slope(scaled)
            h_ref[rows, lanes] = twice_hidden.astype(BF16)
    forward_y(h_ref[...], yf_ref, y_scr)
    spread_x(y_scr, yt_scr, step, x_rows, depth_rows)

    @pl.when(step == pl.num_programs(0) - 1)
    def _():
        forward_depth(zf_ref, yt_scr, out_ref, x_rows)


def final_kernel(q_ref, p_ref, zi_ref, yi_ref, out_ref, z_scr, *, x_rows):
    inverse_depth(q_ref, zi_ref, z_scr, x_rows)
    for group in range(5):
        lanes = slice(256 * group, 256 * group + 256)
        total = inverse_y(z_scr, yi_ref, group) + p_ref[:, lanes].astype(F32)
        out_ref[:, lanes] = total.astype(BF16)


def point_kernel(s_ref, b_ref, out_ref):
    out_ref[...] = dot32(s_ref[...], b_ref[...]).astype(BF16)


def direct_kernel(s_ref, b_ref, bias_ref, out_ref):
    out_ref[...] = ((dot32(s_ref[...], b_ref[...]) + bias_ref[...]) * math.sqrt(0.5)).astype(BF16)


def mode_kernel(
    r_ref, w_ref, gx_ref, perm_ref, u_ref, q_ref,
    in_scr, out_scr, o_scr, ut_scr, u_scr, v_scr, *, backward,
):
    step = pl.program_id(0)
    steps = pl.num_programs(0)
    owners, _, x_groups, modes_here, width = r_ref.shape
    joined = width // CJ
    blocks = [(o, p, g, k) for o in range(owners) for p in range(2) for g in range(x_groups) for k in range(joined)]
    count = modes_here // 2
    cells = 2 * NX
    lane = lax.broadcasted_iota(jnp.int32, (C, 128), 1)
    odd_slot = lane // 32 % 2 == 1
    upper = lane >= 64

    @pl.when(step == 0)
    def _():
        for index, (owner, part, group, k) in enumerate(blocks):
            values = r_ref[owner, part, group, :, CJ * k : CJ * k + CJ].astype(F32)
            for tile in range(4):
                end = min(128 * tile + 128, CJ)
                in_scr[tile, index * modes_here : (index + 1) * modes_here, : end - 128 * tile] = values[
                    :, 128 * tile : end
                ]
        for mode in range(modes_here):
            pair, half = mode // 2, mode % 2
            tiles = [in_scr[tile, pl.ds(mode, cells, stride=modes_here), :] for tile in range(4)]
            block = jnp.concatenate(tiles, axis=1).astype(BF16)
            cols = lax.dot_general(block, gx_ref[...], (((0,), (0,)), ((), ())), preferred_element_type=F32)
            o_scr[half] = cols
            for a in range(6):
                pieces = [o_scr[half, pl.ds(4 * a + r, C, stride=MY), :] for r in range(4)]
                first = jnp.where(odd_slot, pieces[1], pieces[0])
                second = jnp.where(odd_slot, pieces[3], pieces[2])
                lanes = slice(128 * a, 128 * a + 128)
                ut_scr[half, pair, 0, :C, lanes] = jnp.where(upper, pltpu.roll(second, 64, 1), first)
                ut_scr[half, pair, 1, :C, lanes] = jnp.where(upper, second, pltpu.roll(first, 64, 1))
        moved = dot32(ut_scr[...].reshape(2 * count * 48, 768).astype(BF16), perm_ref[...])
        even = moved[: count * 48].reshape(count, 2, 24, 640)
        odd = pltpu.roll(moved[count * 48 :], 64, 1).reshape(count, 2, 24, 640)
        u_scr[:, :, :, :512] = even[:, :, :, :512]
        u_scr[:, :, :, 512:640] = even[:, :, :, 512:] + odd[:, :, :, :128]
        u_scr[:, :, :, 640:] = odd[:, :, :, 128:]

    for sub in range(PAIRS_STEP):
        here = PAIRS_STEP * step + sub
        for part in range(2):
            u_ref[0, part, :, KB * sub : KB * sub + KB] = u_scr[here, part, :C, :].astype(BF16)
        for chunk in range(3):
            lanes = slice(384 * chunk, 384 * chunk + 384)
            w_lanes = slice(KB * sub + 384 * chunk, KB * sub + 384 * chunk + 384)
            if backward:
                real = u_scr[here, 0, :C, lanes]
                imag = u_scr[here, 1, :C, lanes]
                for ch in range(C):
                    w_real = w_ref[0, ch, :, w_lanes].astype(F32)
                    w_imag = w_ref[1, ch, :, w_lanes].astype(F32)
                    v_scr[here, 0, ch : ch + 1, lanes] = jnp.sum(w_real * real + w_imag * imag, axis=0, keepdims=True)
                    v_scr[here, 1, ch : ch + 1, lanes] = jnp.sum(w_real * imag - w_imag * real, axis=0, keepdims=True)
            else:
                real = jnp.zeros((C, 384), F32)
                imag = jnp.zeros((C, 384), F32)
                for ch in range(C):
                    w_real = w_ref[0, ch, :, w_lanes].astype(F32)
                    w_imag = w_ref[1, ch, :, w_lanes].astype(F32)
                    u_real = u_scr[here, 0, ch : ch + 1, lanes]
                    u_imag = u_scr[here, 1, ch : ch + 1, lanes]
                    real = real + w_real * u_real - w_imag * u_imag
                    imag = imag + w_real * u_imag + w_imag * u_real
                v_scr[here, 0, :C, lanes] = real
                v_scr[here, 1, :C, lanes] = imag

    @pl.when(step == steps - 1)
    def _():
        even = v_scr[:, :, :, :640].reshape(count * 48, 640)
        odd = pltpu.roll(v_scr[:, :, :, 512:].reshape(count * 48, 640), 576, 1)
        values = jnp.concatenate([even, odd], axis=0).astype(BF16)
        moved = lax.dot_general(values, perm_ref[...], (((1,), (1,)), ((), ())), preferred_element_type=F32)
        ut_scr[...] = moved.reshape(2, count, 2, 24, 768)
        o_scr[...] = jnp.zeros_like(o_scr)
        for mode in range(modes_here):
            pair, half = mode // 2, mode % 2
            for a in range(6):
                lanes = slice(128 * a, 128 * a + 128)
                real = ut_scr[half, pair, 0, :C, lanes]
                imag = ut_scr[half, pair, 1, :C, lanes]
                first = jnp.where(upper, pltpu.roll(imag, 64, 1), real)
                second = jnp.where(upper, imag, pltpu.roll(real, 64, 1))
                for r, values in enumerate((first, first, second, second)):
                    kept = odd_slot if r % 2 else jnp.logical_not(odd_slot)
                    o_scr[half, pl.ds(4 * a + r, C, stride=MY), :] = jnp.where(kept, values, 0.0)
            back = lax.dot_general(
                gx_ref[...], o_scr[half].astype(BF16), (((1,), (1,)), ((), ())), preferred_element_type=F32
            )
            for tile in range(4):
                out_scr[tile, pl.ds(mode, cells, stride=modes_here), :] = back[:, 128 * tile : 128 * tile + 128]
        for index, (owner, part, group, k) in enumerate(blocks):
            rows = slice(index * modes_here, (index + 1) * modes_here)
            values = jnp.concatenate([out_scr[tile, rows, :] for tile in range(4)], axis=1)
            q_ref[owner, part, group, :, CJ * k : CJ * k + CJ] = values[:, :CJ].astype(BF16)


def weight_kernel(*refs):
    out_ref = refs[-1]
    pieces = refs[:-1]
    width = out_ref.shape[3]
    lane_step = 384 if width % 384 == 0 else width
    row = pl.ds(pl.program_id(0), 1)
    for first in range(0, width, lane_step):
        lanes = slice(first, first + lane_step)
        real = jnp.zeros((C, lane_step), F32)
        imag = jnp.zeros((C, lane_step), F32)
        for u_ref, g_ref in zip(pieces[::2], pieces[1::2]):
            u_real = u_ref[0, row, lanes]
            u_imag = u_ref[1, row, lanes]
            g_real = g_ref[0, :, lanes].astype(F32)
            g_imag = g_ref[1, :, lanes].astype(F32)
            real = real + u_real * g_real + u_imag * g_imag
            imag = imag + u_real * g_imag - u_imag * g_real
        out_ref[0, 0, :, lanes] = real
        out_ref[1, 0, :, lanes] = imag


def cost(micros):
    return pl.CostEstimate(flops=int(micros * 1e9), transcendentals=0, bytes_accessed=int(micros * 3e6))


def whole(_):
    return pl.BlockSpec(memory_space=pltpu.VMEM)


def fixed(array):
    zeros = (0,) * len(array.shape)
    return pl.BlockSpec(array.shape, lambda i: zeros)


def params(mebibytes=52):
    return pltpu.CompilerParams(dimension_semantics=("arbitrary",), vmem_limit_bytes=mebibytes * MIB)


def shape_of(shape, kind):
    return jax.ShapeDtypeStruct(shape, kind)


def local(signal, cotangent, spec_weight, point_weight, bias):
    samples, depth_len, x_rows, merged = signal.shape
    owners = NX // x_rows
    modes_here = MZT // owners
    modes = modes_here * KM
    dp_size = lax.axis_size("dp")
    share = modes // dp_size
    rows_all = ZT * x_rows
    depth_rows = 128
    block = depth_rows * x_rows
    steps = ZT // depth_rows

    forward_np, inverse_np = depth_tables()
    yf_np, yi_np, yi_half_np = y_tiles()
    zf_fwd, zf_inv = jnp.asarray(forward_np), jnp.asarray(inverse_np)
    zi_fwd, zi_inv = jnp.asarray(forward_np.T.reshape(2, ZT, -1)), jnp.asarray(inverse_np.T.reshape(2, ZT, -1))
    yf, yi, yi_half = jnp.asarray(yf_np), jnp.asarray(yi_np), jnp.asarray(yi_half_np)
    yf_half = jnp.asarray((yf_np.astype(np.float32) * 0.5).astype(BF))
    perm = jnp.asarray(lane_perm())
    gx = jnp.asarray(x_table(x_rows))
    spread = jnp.asarray((np.arange(CY)[:, None] // NY == np.arange(C)[None, :]).astype(BF))
    same_y = jnp.asarray(np.arange(NY)[:, None] == np.arange(NY)[None, :])

    sig = signal.reshape(rows_all, CY)
    cot = cotangent.reshape(rows_all, CY)
    joined = math.gcd(x_rows, 4)
    payload = shape_of((owners, 2, x_rows // joined, modes_here, joined * CJ), BF16)
    payload_spec = pl.BlockSpec(payload.shape, lambda i: (0, 0, 0, 0, 0))
    zi_spec = pl.BlockSpec((2, depth_rows, 2 * MZT), lambda i: (0, i, 0))
    row_spec = pl.BlockSpec((block, CY), lambda i: (i, 0))
    y_scr = pltpu.VMEM((8, block, 128), F32)
    yt_scr = pltpu.VMEM((x_rows, 2 * ZT, LANES), BF16)
    z_scr = pltpu.VMEM((8, block, 128), F32)
    sizes = dict(x_rows=x_rows, depth_rows=depth_rows)

    def point_block(weights):
        wide = dot32(dot32(spread, weights).astype(BF16), spread.T)
        row_y = lax.broadcasted_iota(jnp.int32, (CY, CY), 0) % NY
        col_y = lax.broadcasted_iota(jnp.int32, (CY, CY), 1) % NY
        return jnp.where(row_y == col_y, wide, 0.0).astype(BF16)

    def point(kernel, values, weights, *rest):
        matrix = point_block(weights)
        return pl.pallas_call(
            kernel,
            grid=(steps,),
            in_specs=[row_spec, whole(matrix)] + [whole(array) for array in rest],
            out_specs=row_spec,
            out_shape=shape_of((rows_all, CY), BF16),
            compiler_params=params(), cost_estimate=cost(18),
            name="point",
        )(values, matrix, *rest)

    width = PAIRS_STEP * KB
    aligned = share % width == 0

    def modes_call(received, backward):
        pairs = modes_here // 2
        if aligned:
            per = share // width
            u_shape = shape_of((dp_size, 2, C, share), BF16)
            u_spec = pl.BlockSpec((1, 2, C, width), lambda i: (i // per, 0, 0, i % per))
        else:
            u_shape = shape_of((1, 2, C, modes), BF16)
            u_spec = pl.BlockSpec((1, 2, C, width), lambda i: (0, 0, 0, i))
        return pl.pallas_call(
            functools.partial(mode_kernel, backward=backward),
            grid=(pairs // PAIRS_STEP,),
            in_specs=[
                whole(received),
                pl.BlockSpec((2, C, C, width), lambda i: (0, 0, 0, i)),
                whole(gx),
                whole(perm),
            ],
            out_specs=(u_spec, payload_spec),
            out_shape=(u_shape, payload),
            scratch_shapes=[
                pltpu.VMEM((4, 2 * NX * modes_here, 128), F32),
                pltpu.VMEM((4, 2 * NX * modes_here, 128), F32),
                pltpu.VMEM((2, LANES, 128), F32),
                pltpu.VMEM((2, pairs, 2, 24, 768), F32),
                pltpu.VMEM((pairs, 2, 24, KB), F32),
                pltpu.VMEM((pairs, 2, 24, KB), F32),
            ],
            compiler_params=params(46), cost_estimate=cost(27),
            name="modes",
        )(received, spec_weight, gx, perm)

    def exchange(values):
        return lax.all_to_all(values, "space", split_axis=0, concat_axis=0, tiled=True)

    me = lax.axis_index("dp")

    def to_owners(spectrum):
        if aligned:
            cut = spectrum
        else:
            cut = jnp.transpose(spectrum[0].reshape(2, C, dp_size, share), (2, 0, 1, 3))
        pieces = []
        for shift in range(dp_size):
            piece = lax.dynamic_index_in_dim(cut, (me + shift) % dp_size, 0, keepdims=False)
            if shift:
                piece = lax.ppermute(piece, "dp", [(i, (i + shift) % dp_size) for i in range(dp_size)])
            pieces.append(piece)
        return pieces

    coeffs = pl.pallas_call(
        functools.partial(analyse_kernel, **sizes),
        grid=(steps,),
        in_specs=[row_spec, fixed(yf), fixed(zf_fwd)],
        out_specs=payload_spec,
        out_shape=payload,
        scratch_shapes=[y_scr, yt_scr],
        compiler_params=params(62), cost_estimate=cost(14),
        name="analyse",
    )(sig, yf, zf_fwd)
    bias_row = jnp.repeat(bias.astype(F32), NY).reshape(1, CY)
    direct = point(direct_kernel, sig, point_weight, bias_row)
    received, direct = lax.optimization_barrier((exchange(coeffs), direct))
    u_hat, v_cells = modes_call(received, False)
    u_pieces = [piece.astype(F32) for piece in to_owners(u_hat)]
    v_here, u_pieces = lax.optimization_barrier((exchange(v_cells), u_pieces))
    twice_hidden, e_coeffs = pl.pallas_call(
        functools.partial(middle_kernel, **sizes),
        grid=(steps,),
        in_specs=[
            whole(payload), row_spec, row_spec, zi_spec, whole(yi_half), whole(yf_half), fixed(zf_inv),
        ],
        out_specs=(row_spec, payload_spec),
        out_shape=(shape_of((rows_all, CY), BF16), payload),
        scratch_shapes=[z_scr, y_scr, yt_scr],
        compiler_params=params(), cost_estimate=cost(32),
        name="middle",
    )(v_here, direct, cot, zi_inv, yi_half, yf_half, zf_inv)
    pointwise = point(point_kernel, twice_hidden, point_weight.T * 0.5)
    received, pointwise = lax.optimization_barrier((exchange(e_coeffs), pointwise))
    g_hat, d_cells = modes_call(received, True)
    d_here = exchange(d_cells)
    grad_signal = pl.pallas_call(
        functools.partial(final_kernel, x_rows=x_rows),
        grid=(steps,),
        in_specs=[whole(payload), row_spec, zi_spec, whole(yi)],
        out_specs=row_spec,
        out_shape=shape_of((rows_all, CY), BF16),
        scratch_shapes=[z_scr],
        compiler_params=params(), cost_estimate=cost(16),
        name="final",
    )(d_here, pointwise, zi_fwd, yi)
    pieces = [piece for pair in zip(u_pieces, to_owners(g_hat)) for piece in pair]
    spec_grad = pl.pallas_call(
        weight_kernel,
        grid=(C,),
        in_specs=[whole(piece) for piece in pieces],
        out_specs=pl.BlockSpec((2, 1, C, share), lambda i: (0, i, 0, 0)),
        out_shape=shape_of((2, C, C, share), F32),
        compiler_params=params(), cost_estimate=cost(13),
        name="weight",
    )(*pieces)
    return (grad_signal.reshape(signal.shape), spec_grad)


def solution(mesh):
    return jax.shard_map(
        local,
        mesh=mesh,
        in_specs=(
            P("dp", None, "space", None),
            P("dp", None, "space", None),
            P(None, None, None, "space"),
            P(),
            P(),
        ),
        out_specs=(P("dp", None, "space", None), P(None, None, None, ("space", "dp"))),
        check_vma=False,
    )
```
